128 devices in a mesh: path: 4 (over z_lo, core), ctx: 32 (over x, z_hi, y).
Axes of the slice: x: 4, y: 4, z: 4 (z_hi: 2, z_lo: 2; z = z_hi * 2 + z_lo), core: 2. Of those that a mesh axis runs over, the one named last changes fastest.
Arguments:
- tokens: int32 [4096], P('ctx'), may hold values from 0 to 511
- sub_pos: int32 [512], P('ctx'), may hold values from 0 to 4095, as said below
- sub_base: int32 [512], P('ctx'), may hold values from 0 to 511
- embed: bfloat16 [512, 4096], replicated, may hold values from -6 to 6
- norm_gain: float32 [4096], replicated, may hold values from 0.1 to 1.9
- fir_taps: bfloat16 [3, 3, 4096], replicated, may hold values from -3.5 to 3.5
- long_filter: float32 [4096, 4096], P(None, 'ctx'), may hold values from -8 to 8
- skip_gain: float32 [4096], P('ctx'), may hold values from 0.5 to 1.5
- cotangent: bfloat16 [4096, 4096], P('ctx'), may hold values from -6 to 6
Outputs:
- path_grad: float32 [4096, 4096], P('ctx', 'path')
- attribution: float32 [4096, 4096], P('ctx', 'path')
The draws below stay inside these ranges and needn't reach their ends.
Inputs may be any that keep to these rules, and one draw needn't show every extreme that they name: `sub_pos`: exactly one substituted position in each aligned block of 8 tokens, so the positions rise strictly.
All inputs are finite; a program needn't handle non-finite values.
Results may differ from the reference program's by a relative error of at most 0.0085.
Values may be sent and summed in bfloat16 or wider, within the bound.
A program may use at most 192 MiB of HBM per device.

```python
import jax
import jax.numpy as jnp
from jax import lax

D = 4096
VOCAB = 512
FIR_TAPS = 3
TOKENS = 4096
PATHS = 4
SUBS = 512


def substitution_draw(key):
    token_ids = jax.random.randint(jax.random.fold_in(key, 11), (TOKENS,), 0, VOCAB, dtype=jnp.int32)
    offsets = jax.random.randint(jax.random.fold_in(key, 3), (SUBS,), 0, 8, dtype=jnp.int32)
    positions = (jnp.arange(SUBS, dtype=jnp.int32) * 8 + offsets).astype(jnp.int32)
    chosen = jnp.take(token_ids, positions, axis=0)
    partner = ((chosen + VOCAB // 2) % VOCAB).astype(jnp.int32)
    return (token_ids, positions, partner)


def draw_tokens(key, part):
    return substitution_draw(key)[0]


def draw_sub_pos(key, part):
    return substitution_draw(key)[1]


def draw_sub_base(key, part):
    return substitution_draw(key)[2]


def draw_embed(key, part):
    half = VOCAB // 2
    lead_key, extra_key = jax.random.split(jax.random.fold_in(key, 19))
    lead = jnp.clip(jax.random.normal(lead_key, (half, D), jnp.float32), -4.0, 4.0)
    extra = jnp.clip(jax.random.normal(extra_key, (half, D), jnp.float32), -4.0, 4.0)
    partner = -0.5 * lead + 0.1 * extra
    return jnp.concatenate([lead, partner], 0).astype(jnp.bfloat16)


def draw_long_filter(key, part):
    jitter_key, decay_key = jax.random.split(jax.random.fold_in(key, 7))
    jitter = jnp.clip(jax.random.normal(jitter_key, (TOKENS, D), jnp.float32), -6.0, 6.0)
    lowest = 30.0
    decay_len = jnp.exp(jax.random.uniform(decay_key, (D,), jnp.float32, jnp.log(lowest), jnp.log(4.0 * TOKENS)))
    position = jnp.arange(TOKENS, dtype=jnp.float32)[:, None]
    envelope = jnp.exp(-position / decay_len[None, :])
    return jitter * envelope / jnp.sqrt(jnp.sum(envelope * envelope, 0, keepdims=True))


def block_levels(rng, dims, shards, smallest, largest):
    gain, own = 1.0, jax.random.fold_in(rng, 6)
    for dim, shards_of in shards:
        steps = jnp.exp(jax.random.uniform(jax.random.fold_in(own, dim), (shards_of,), jnp.float32, smallest / len(shards), largest / len(shards)))
        gain = gain * jnp.repeat(steps, dims[dim] // shards_of).reshape([-1 if axis == dim else 1 for axis in range(len(dims))])
    return gain


def normal_values(stream_key, shape, scale, bound, cuts=(), kind=jnp.bfloat16):
    result = jax.random.normal(stream_key, shape, jnp.float32) * scale
    if len(cuts) > 0:
        result = block_levels(stream_key, shape, cuts, -0.22, 0.18) * result
    return jnp.clip(result, min=-bound, max=bound).astype(kind)


def setup_inputs(seed: int = 0) -> dict:
    keys = jax.random.split(jax.random.key(seed), 10)
    tokens = draw_tokens(jax.random.fold_in(keys[9], 71), 0)
    sub_pos = draw_sub_pos(jax.random.fold_in(keys[9], 71), 0)
    sub_base = draw_sub_base(jax.random.fold_in(keys[9], 71), 0)
    embed = draw_embed(jax.random.fold_in(keys[9], 71), 0)
    norm_gain = jnp.clip(1.0 + 0.18 * jax.random.normal(keys[4], (D,), jnp.float32), 0.1, 1.9)
    fir_taps = normal_values(keys[5], (3, FIR_TAPS, D), FIR_TAPS ** -0.5, 3.5)
    long_filter = draw_long_filter(jax.random.fold_in(keys[9], 71), 0)
    skip_gain = jnp.clip(0.5 + 1.0 * jax.random.uniform(keys[7], (D,), jnp.float32) ** block_levels(keys[7], (D,), ((0, 32),), -0.2, 0.2), 0.5, 1.5)
    cotangent = normal_values(keys[8], (TOKENS, D), 1.0, 6.0, ((0, 32),))
    return dict(tokens=tokens, sub_pos=sub_pos, sub_base=sub_base, embed=embed, norm_gain=norm_gain, fir_taps=fir_taps, long_filter=long_filter, skip_gain=skip_gain, cotangent=cotangent)


def rounded(value):
    return lax.optimization_barrier(value.astype(jnp.bfloat16)).astype(jnp.float32)

def causal(signal, filters):
    length = signal.shape[0] + filters.shape[0]
    product = jnp.fft.rfft(signal, n=length, axis=0) * jnp.fft.rfft(filters, n=length, axis=0)
    return jnp.fft.irfft(product, n=length, axis=0)[:signal.shape[0]]

def anticausal(signal, filters):
    length = signal.shape[0] + filters.shape[0]
    product = jnp.fft.rfft(signal, n=length, axis=0) * jnp.conj(jnp.fft.rfft(filters, n=length, axis=0))
    return jnp.fft.irfft(product, n=length, axis=0)[:signal.shape[0]]

def reference(tokens, sub_pos, sub_base, embed, norm_gain, fir_taps, long_filter, skip_gain, cotangent):
    base_ids = tokens.at[sub_pos].set(sub_base)
    emb_tok = embed[tokens].astype(jnp.float32)
    emb_base = embed[base_ids].astype(jnp.float32)
    difference = emb_tok - emb_base
    filters = fir_taps.astype(jnp.float32)
    upstream = cotangent.astype(jnp.float32)

    def one_point(total, point):
        alpha = (point.astype(jnp.float32) + 0.5) / PATHS
        inputs = emb_base + alpha * difference
        inv_rms = lax.rsqrt(lax.optimization_barrier(jnp.mean(inputs * inputs, -1, keepdims=True)) + 1e-06)
        normed = rounded(inputs * inv_rms * norm_gain)
        q_feat = causal(normed, filters[0])
        k_feat = causal(normed, filters[1])
        v_feat = causal(normed, filters[2])
        gated = rounded(k_feat * v_feat)
        conv_out = rounded(causal(gated, long_filter) + skip_gain * gated)
        grad_q = rounded(upstream * conv_out)
        grad_y = rounded(upstream * q_feat)
        grad_z = rounded(anticausal(grad_y, long_filter) + skip_gain * grad_y)
        grad_k = rounded(grad_z * v_feat)
        grad_v = rounded(grad_z * k_feat)
        grad_norm = anticausal(grad_q, filters[0]) + anticausal(grad_k, filters[1]) + anticausal(grad_v, filters[2])
        scaled = norm_gain * grad_norm
        grad_in = inv_rms * scaled - inputs * inv_rms ** 3 * lax.optimization_barrier(jnp.mean(inputs * scaled, -1, keepdims=True))
        return (total + grad_in, None)
    total = lax.scan(one_point, jnp.zeros((TOKENS, D), jnp.float32), jnp.arange(PATHS, dtype=jnp.int32))[0]
    path_grad = total / PATHS
    return (path_grad, difference * path_grad)
```

```python
import functools

import jax
import jax.numpy as jnp
from jax import lax
from jax.experimental import pallas as pl
from jax.experimental.pallas import tpu as pltpu
from jax.sharding import PartitionSpec as P

MESH = pl.DeviceIdType.MESH
F32 = jnp.float32
BF16 = jnp.bfloat16

NP = 4
NC = 32
TB = 128
CH = 32
NB = 32
SUB = 16
VOCAB = 512
D = 4096
REACH = 2
ALPHAS = tuple((a + 0.5) / NP for a in range(NP))
VMEM_LIMIT = 60 * 1024 * 1024


def iota(shape, dim):
    return lax.broadcasted_iota(jnp.int32, shape, dim)


def rounded(x):
    return x.astype(BF16).astype(F32)


def nt_dot(a, b):
    return lax.dot_general(a, b, (((1,), (1,)), ((), ())), preferred_element_type=F32)


def gather_kernel(
    tok_ref,
    sub_pos_ref,
    sub_base_ref,
    embed_ref,
    cot_ref,
    info_ref,
    cols_ref,
    mine,
    parts,
    info_send,
    info_recv,
    cols_send,
    cols_recv,
    own_sem,
):
    path = lax.axis_index("path")
    me = lax.axis_index("ctx")

    barrier = pltpu.get_barrier_semaphore()

    @pl.loop(1, NC)
    def _(d):
        pl.semaphore_signal(
            barrier, inc=1, device_id={"ctx": lax.rem(me + d, NC)}, device_id_type=MESH
        )

    pick = (iota((CH, TB), 1) == iota((CH, TB), 0) + path * CH).astype(F32).astype(BF16)

    @pl.loop(0, NC)
    def _(j):
        block = cot_ref[:, pl.ds(pl.multiple_of(j * TB, TB), TB)]
        parts[j] = nt_dot(pick, block).astype(BF16)

    pl.semaphore_wait(barrier, NC - 1)

    def cols_copy(d, dst, slot):
        return pltpu.make_async_remote_copy(
            src_ref=parts.at[dst],
            dst_ref=cols_ref.at[slot],
            send_sem=cols_send.at[d],
            recv_sem=cols_recv.at[d],
            device_id={"ctx": dst},
            device_id_type=MESH,
        )

    def info_copy(d, dst, slot):
        return pltpu.make_async_remote_copy(
            src_ref=mine,
            dst_ref=info_ref.at[slot],
            send_sem=info_send.at[d],
            recv_sem=info_recv.at[d],
            device_id={"ctx": dst},
            device_id_type=MESH,
        )

    @pl.loop(1, NC)
    def _(d):
        cols_copy(d, lax.rem(me + d, NC), me).start()

    own_cols = pltpu.make_async_copy(parts.at[me], cols_ref.at[me], own_sem.at[0])
    own_cols.start()

    tok = tok_ref[...].astype(F32)
    diag = iota((SUB, SUB), 0) == iota((SUB, SUB), 1)
    pos_row = (sub_pos_ref[...] & 7).astype(F32)
    pos_col = jnp.sum(jnp.where(diag, pos_row, 0.0), 1, keepdims=True) + 8.0 * iota(
        (SUB, 1), 0
    ).astype(F32)
    base_col = jnp.sum(jnp.where(diag, sub_base_ref[...].astype(F32), 0.0), 1, keepdims=True)
    at_sub = iota((SUB, TB), 1).astype(F32) == pos_col
    covered = jnp.sum(jnp.where(at_sub, 1.0, 0.0), 0, keepdims=True) > 0.5
    base = jnp.where(
        covered, jnp.sum(jnp.where(at_sub, base_col, 0.0), 0, keepdims=True), tok
    )
    sub_tok_col = jnp.sum(jnp.where(at_sub, tok, 0.0), 1, keepdims=True)
    eye = iota((TB, TB), 0) == iota((TB, TB), 1)
    tok_col = jnp.sum(jnp.where(eye, tok, 0.0), 1, keepdims=True)
    ids = jnp.concatenate([tok_col, sub_tok_col, base_col], 0)
    rows = TB + 2 * SUB
    hot = (iota((rows, VOCAB), 1).astype(F32) == ids).astype(F32).astype(BF16)

    def squares(step, carry):
        plain, subs = carry
        part = embed_ref[:, pl.ds(pl.multiple_of(step * 256, 256), 256)]
        found = jnp.dot(hot, part, preferred_element_type=F32)
        own = found[:TB]
        own = own * own
        plain = plain + own[:, :TB] + own[:, TB:]
        e_tok = found[TB : TB + SUB]
        e_base = found[TB + SUB :]
        diff = e_tok - e_base
        new = []
        for a in range(NP):
            x = e_base + ALPHAS[a] * diff
            x = x * x
            new.append(subs[a] + x[:, :TB] + x[:, TB:])
        return plain, tuple(new)

    plain, subs = lax.fori_loop(
        0,
        D // 256,
        squares,
        (jnp.zeros((TB, TB), F32), tuple(jnp.zeros((SUB, TB), F32) for _ in range(NP))),
    )

    def inverse(total):
        return lax.rsqrt(jnp.sum(total, 1, keepdims=True) / D + 1e-06)

    plain_row = jnp.sum(jnp.where(eye, inverse(plain), 0.0), 0, keepdims=True)
    for a in range(NP):
        sub_row = jnp.sum(jnp.where(at_sub, inverse(subs[a]), 0.0), 0, keepdims=True)
        mine[a : a + 1, :] = jnp.where(covered, sub_row, plain_row)
    mine[4:5, :] = tok
    mine[5:6, :] = base
    mine[6:8, :] = jnp.zeros((2, TB), F32)

    @pl.loop(1, NC)
    def _(d):
        info_copy(d, lax.rem(me + d, NC), me).start()

    own_info = pltpu.make_async_copy(mine, info_ref.at[me], own_sem.at[1])
    own_info.start()

    @pl.loop(1, NC)
    def _(d):
        dst = lax.rem(me + d, NC)
        src = lax.rem(me - d + NC, NC)
        cols_copy(d, dst, src).wait_recv()
        info_copy(d, dst, src).wait_recv()
        cols_copy(d, dst, me).wait_send()
        info_copy(d, dst, me).wait_send()

    own_cols.wait()
    own_info.wait()


def gather_stage(tokens, sub_pos, sub_base, embed, cotangent):
    vmem = pl.BlockSpec(memory_space=pltpu.VMEM)
    return pl.pallas_call(
        gather_kernel,
        name="gather_stage",
        out_shape=(
            jax.ShapeDtypeStruct((NC, 8, TB), F32),
            jax.ShapeDtypeStruct((NC, CH, TB), BF16),
        ),
        in_specs=[vmem] * 5,
        out_specs=(vmem, vmem),
        scratch_shapes=[
            pltpu.VMEM((8, TB), F32),
            pltpu.VMEM((NC, CH, TB), BF16),
            pltpu.SemaphoreType.DMA((NC,)),
            pltpu.SemaphoreType.DMA((NC,)),
            pltpu.SemaphoreType.DMA((NC,)),
            pltpu.SemaphoreType.DMA((NC,)),
            pltpu.SemaphoreType.DMA((2,)),
        ],
        compiler_params=pltpu.CompilerParams(
            collective_id=0, has_side_effects=True, vmem_limit_bytes=VMEM_LIMIT
        ),
    )(tokens.reshape(1, -1), sub_pos.reshape(1, -1), sub_base.reshape(1, -1), embed, cotangent)


def take_lanes(table, index):
    rows = table.shape[0]
    low = jnp.broadcast_to(index & (TB - 1), (8, TB))
    high = jnp.broadcast_to(index >> 7, (8, TB))
    out = []
    for r in range(0, rows, 8):
        got = jnp.take_along_axis(table[r : r + 8, :TB], low, axis=1)
        for v in range(1, VOCAB // TB):
            more = jnp.take_along_axis(table[r : r + 8, v * TB : (v + 1) * TB], low, axis=1)
            got = jnp.where(high == v, more, got)
        out.append(got)
    return jnp.concatenate(out, 0)


def channel_kernel(
    path_index,
    ctx_index,
    info_ref,
    cols_ref,
    embed_ref,
    gain_ref,
    taps_ref,
    filter_ref,
    skip_ref,
    out_ref,
    ab_ref,
    emb_buf,
    table,
    taps,
    coef,
    time_filter,
    e_base_s,
    diff_s,
    key_s,
    val_s,
    stage,
    conv,
    past,
    pairs,
    toeplitz,
    acc,
    ahead,
    sem,
):
    path = path_index()
    ctx = ctx_index()
    lanes = pl.ds(pl.multiple_of(ctx * TB, TB), TB)
    load = pltpu.make_async_copy(embed_ref.at[:, lanes], emb_buf, sem)
    load.start()

    lane = iota((CH, TB), 1)
    chosen = lane == iota((CH, TB), 0) + path * CH
    pick = chosen.astype(F32).astype(BF16)

    def column(row):
        return jnp.broadcast_to(
            jnp.sum(jnp.where(chosen, row, 0.0), 1, keepdims=True), (CH, TB)
        )

    coef[0] = column(gain_ref[pl.ds(ctx, 1), :])
    coef[1] = column(skip_ref[...])
    for f in range(3):
        for j in range(3):
            taps[f * 3 + j] = column(taps_ref[f, j : j + 1, lanes].astype(F32))

    @pl.loop(0, NB)
    def _(k):
        part = filter_ref[pl.ds(pl.multiple_of(k * TB, TB), TB), :].astype(BF16)
        time_filter[k] = nt_dot(pick, part)

    load.wait()
    table[...] = nt_dot(pick, emb_buf[...])

    flip = (iota((TB, TB), 0) + iota((TB, TB), 1) == TB - 1).astype(F32).astype(BF16)
    past[...] = jnp.zeros_like(past)

    def forward(a, _):
        info = info_ref[a]
        e_tok = take_lanes(table[...], info[4:5].astype(jnp.int32))
        e_base = take_lanes(table[...], info[5:6].astype(jnp.int32))
        diff = e_tok - e_base
        e_base_s[a] = e_base
        diff_s[a] = diff
        cot = cols_ref[a].astype(F32)
        gain = coef[0]
        grads = []
        for p in range(NP):
            now = rounded((e_base + ALPHAS[p] * diff) * info[p : p + 1] * gain)
            one = pltpu.roll(now, 1, 1)
            two = pltpu.roll(now, 2, 1)
            now1 = jnp.where(lane < 1, past[p, 0], one)
            now2 = jnp.where(lane < 2, past[p, 1], two)
            past[p, 0] = one
            past[p, 1] = two
            q, k, v = (
                taps[f * 3] * now + taps[f * 3 + 1] * now1 + taps[f * 3 + 2] * now2
                for f in range(3)
            )
            key_s[a, p] = k
            val_s[a, p] = v
            stage[a, p * CH : (p + 1) * CH, :] = rounded(k * v)
            grads.append((cot * q).astype(BF16))
        turned = jnp.dot(jnp.concatenate(grads, 0), flip, preferred_element_type=F32)
        stage[NB - 1 - a, NP * CH :, :] = turned
        return 0

    lax.fori_loop(0, NB, forward, 0)

    lane8 = iota((16, TB), 1)
    sub8 = iota((16, TB), 0)

    def channel(c, _):
        rows = pl.ds(c, 8, stride=CH)
        last = jnp.zeros((8, TB), F32)
        for t in range(NB // 2):
            low = stage[2 * t, rows, :]
            high = stage[2 * t + 1, rows, :]
            pairs[16 * t : 16 * t + 16, :TB] = jnp.concatenate([low, high], 0).astype(BF16)
            pairs[16 * t : 16 * t + 16, TB:] = jnp.concatenate([last, low], 0).astype(BF16)
            last = high

        before = jnp.zeros((16, TB), F32)
        shear_before = jnp.zeros((16, TB), BF16)
        for k in range(NB):
            row = jnp.broadcast_to(time_filter[k, pl.ds(c, 1), :], (16, TB))
            turned = pltpu.roll(row, 0, 1, stride=1, stride_axis=0)
            shear = jnp.where(lane8 >= sub8, turned, before).astype(BF16)
            before = turned
            for g in range(TB // 16):
                if g == 0:
                    tile = shear
                else:
                    tile = jnp.concatenate(
                        [shear_before[:, TB - 16 * g :], shear[:, : TB - 16 * g]], 1
                    )
                toeplitz[TB * k + 16 * g : TB * k + 16 * g + 16, :] = tile
            shear_before = shear

        for s in range(NB // 2):
            size = 256 - 16 * s
            part = jnp.dot(
                pairs[:size], toeplitz[256 * s : 256 * s + 256], preferred_element_type=F32
            )
            if s == 0:
                acc[...] = part
            else:
                acc[16 * s :] += part
        for a in range(NB):
            conv[a, rows, :] = acc[8 * a : 8 * a + 8, :]
        return 0

    lax.fori_loop(0, CH, channel, 0)

    ahead[...] = jnp.zeros_like(ahead)

    def backward(step, _):
        a = NB - 1 - step
        info = info_ref[a]
        cot = cols_ref[a].astype(F32)
        e_base = e_base_s[a]
        diff = diff_s[a]
        gain = coef[0]
        skip = coef[1]
        turned = []
        for p in range(NP):
            rows = slice((NP + p) * CH, (NP + p + 1) * CH)
            turned.append(
                (conv[step, rows, :] + skip * stage[step, rows, :]).astype(BF16)
            )
        grad_z = jnp.dot(jnp.concatenate(turned, 0), flip, preferred_element_type=F32)
        total = jnp.zeros((CH, TB), F32)
        sum_a = jnp.zeros((CH, TB), F32)
        sum_b = jnp.zeros((CH, TB), F32)
        for p in range(NP):
            rows = slice(p * CH, (p + 1) * CH)
            out = rounded(conv[a, rows, :] + skip * stage[a, rows, :])
            gz = grad_z[rows]
            gq = rounded(cot * out)
            gk = rounded(gz * val_s[a, p])
            gv = rounded(gz * key_s[a, p])
            u0, u1, u2 = (taps[j] * gq + taps[3 + j] * gk + taps[6 + j] * gv for j in range(3))
            one = pltpu.roll(u1, TB - 1, 1)
            two = pltpu.roll(u2, TB - 2, 1)
            gn = (
                u0
                + jnp.where(lane < TB - 1, one, ahead[p, 0])
                + jnp.where(lane < TB - 2, two, ahead[p, 1])
            )
            ahead[p, 0] = one
            ahead[p, 1] = two
            inv = info[p : p + 1]
            scaled = gain * gn
            total = total + inv * scaled
            w = (e_base + ALPHAS[p] * diff) * scaled * (inv * inv * inv)
            sum_a = sum_a + w
            sum_b = sum_b + ALPHAS[p] * w
        out_ref[a] = total.astype(BF16)
        ab_ref[a, 0:1, :] = jnp.sum(sum_a, 0, keepdims=True)
        ab_ref[a, 1:2, :] = jnp.sum(sum_b, 0, keepdims=True)
        ab_ref[a, 2:8, :] = jnp.zeros((6, TB), F32)
        return 0

    lax.fori_loop(0, NB, backward, 0)


def axis_path():
    return lax.axis_index("path")


def axis_ctx():
    return lax.axis_index("ctx")


def channel_stage(
    info, cols, embed, gain, taps, long_filter, skip, path_index=axis_path, ctx_index=axis_ctx
):
    vmem = pl.BlockSpec(memory_space=pltpu.VMEM)
    return pl.pallas_call(
        functools.partial(channel_kernel, path_index, ctx_index),
        name="channel_stage",
        out_shape=(
            jax.ShapeDtypeStruct((NB, CH, TB), BF16),
            jax.ShapeDtypeStruct((NB, 8, TB), F32),
        ),
        in_specs=[vmem, vmem, pl.BlockSpec(memory_space=pl.ANY), vmem, vmem, vmem, vmem],
        out_specs=(vmem, vmem),
        scratch_shapes=[
            pltpu.VMEM((VOCAB, TB), BF16),
            pltpu.VMEM((CH, VOCAB), F32),
            pltpu.VMEM((9, CH, TB), F32),
            pltpu.VMEM((2, CH, TB), F32),
            pltpu.VMEM((NB, CH, TB), F32),
            pltpu.VMEM((NB, CH, TB), F32),
            pltpu.VMEM((NB, CH, TB), F32),
            pltpu.VMEM((NB, NP, CH, TB), F32),
            pltpu.VMEM((NB, NP, CH, TB), F32),
            pltpu.VMEM((NB, 2 * NP * CH, TB), F32),
            pltpu.VMEM((NB, 2 * NP * CH, TB), F32),
            pltpu.VMEM((NP, 2, CH, TB), F32),
            pltpu.VMEM((256, 256), BF16),
            pltpu.VMEM((NB * TB, TB), BF16),
            pltpu.VMEM((256, TB), F32),
            pltpu.VMEM((NP, 2, CH, TB), F32),
            pltpu.SemaphoreType.DMA,
        ],
        compiler_params=pltpu.CompilerParams(vmem_limit_bytes=VMEM_LIMIT),
    )(info, cols, embed, gain.reshape(-1, TB), taps, long_filter, skip.reshape(1, -1))


def output_kernel(
    sums_ref,
    ab_ref,
    info_ref,
    embed_ref,
    grad_ref,
    attr_ref,
    got,
    got_ab,
    group_ab,
    own_ab,
    emb_buf,
    base_s,
    diff_s,
    sums_send,
    sums_recv,
    ab_send,
    ab_recv,
    group_send,
    group_recv,
    own_sem,
):
    path = lax.axis_index("path")
    me = lax.axis_index("ctx")
    width = D // NP
    load = pltpu.make_async_copy(
        embed_ref.at[:, pl.ds(pl.multiple_of(path * width, width), width)], emb_buf, own_sem.at[2]
    )
    load.start()
    barrier = pltpu.get_barrier_semaphore()
    to_path = me // 8
    slot = (me % 8) * NP + path
    own = jnp.where(to_path == path, 1, 0)

    @pl.loop(0, NC)
    def _(s):
        src_path = lax.rem(s, NP)
        src_ctx = path * 8 + s // NP

        @pl.when((src_path != path) | (src_ctx != me))
        def _():
            pl.semaphore_signal(
                barrier,
                inc=1,
                device_id={"path": src_path, "ctx": src_ctx},
                device_id_type=MESH,
            )

    @pl.loop(1, NP)
    def _(d):
        pl.semaphore_signal(
            barrier, inc=1, device_id={"path": lax.rem(path + d, NP)}, device_id_type=MESH
        )

    pl.semaphore_wait(barrier, NC + NP - 1 - own)

    def sums_copy(dst, at, number):
        return pltpu.make_async_remote_copy(
            src_ref=sums_ref.at[dst],
            dst_ref=got.at[at],
            send_sem=sums_send.at[dst],
            recv_sem=sums_recv.at[number],
            device_id={"path": to_path, "ctx": dst},
            device_id_type=MESH,
        )

    def ab_copy(dst, at, number):
        return pltpu.make_async_remote_copy(
            src_ref=ab_ref.at[dst],
            dst_ref=got_ab.at[at],
            send_sem=ab_send.at[dst],
            recv_sem=ab_recv.at[number],
            device_id={"path": to_path, "ctx": dst},
            device_id_type=MESH,
        )

    def group_copy(d, at):
        return pltpu.make_async_remote_copy(
            src_ref=own_ab,
            dst_ref=group_ab.at[at],
            send_sem=group_send.at[d],
            recv_sem=group_recv.at[d],
            device_id={"path": lax.rem(path + d, NP)},
            device_id_type=MESH,
        )

    def is_self(dst):
        return (to_path == path) & (dst == me)

    own_sums = pltpu.make_async_copy(sums_ref.at[me], got.at[slot], own_sem.at[0])
    own_part = pltpu.make_async_copy(ab_ref.at[me], got_ab.at[slot], own_sem.at[1])

    @pl.when(to_path == path)
    def _():
        own_sums.start()
        own_part.start()

    @pl.loop(0, NC)
    def _(d):
        dst = lax.rem(me + d, NC)

        @pl.when(jnp.logical_not(is_self(dst)))
        def _():
            ab_copy(dst, slot, slot).start()
            sums_copy(dst, slot, slot).start()

    load.wait()
    info = info_ref[pl.ds(me, 1)][0]
    eye = iota((TB, TB), 0) == iota((TB, TB), 1)
    unit = eye.astype(F32).astype(BF16)

    def as_column(row):
        return jnp.sum(jnp.where(eye, row, 0.0), 1, keepdims=True)

    vocab = iota((TB, VOCAB), 1).astype(F32)
    hot_tok = (vocab == as_column(info[4:5])).astype(F32).astype(BF16)
    hot_base = (vocab == as_column(info[5:6])).astype(F32).astype(BF16)

    @pl.loop(0, width // 256)
    def _(s):
        columns = pl.ds(pl.multiple_of(s * 256, 256), 256)
        part = emb_buf[:, columns]
        e_tok = jnp.dot(hot_tok, part, preferred_element_type=F32)
        e_base = jnp.dot(hot_base, part, preferred_element_type=F32)
        base_s[:, columns] = e_base
        diff_s[:, columns] = e_tok - e_base

    self_slot = (me % 8) * NP + path

    def others(s):
        return jnp.logical_not((to_path == path) & (s == self_slot))

    @pl.loop(0, NC)
    def _(s):
        @pl.when(others(s))
        def _():
            ab_copy(me, s, s).wait_recv()

    @pl.when(to_path == path)
    def _():
        own_part.wait()

    own_ab[...] = jnp.sum(got_ab[...], 0)

    @pl.loop(1, NP)
    def _(d):
        group_copy(d, path).start()

    @pl.loop(0, NC)
    def _(s):
        @pl.when(others(s))
        def _():
            sums_copy(me, s, s).wait_recv()

    @pl.when(to_path == path)
    def _():
        own_sums.wait()

    ab = own_ab[...]
    for d in range(1, NP):
        src = lax.rem(path - d + NP, NP)
        group_copy(d, src).wait_recv()
        ab = ab + group_ab[pl.ds(src, 1)][0]
    scale = 1.0 / (NP * D)
    a_col = as_column(ab[0:1]) * scale
    b_col = as_column(ab[1:2]) * scale

    @pl.loop(0, width // TB)
    def _(s):
        columns = pl.ds(pl.multiple_of(s * TB, TB), TB)
        block = got[pl.ds(s * 4, 4)].reshape(TB, TB)
        summed = nt_dot(unit, block)
        diff = diff_s[:, columns]
        grad = summed * (1.0 / NP) - (base_s[:, columns] * a_col + diff * b_col)
        grad_ref[:, columns] = grad
        attr_ref[:, columns] = diff * grad

    @pl.loop(0, NC)
    def _(d):
        dst = lax.rem(me + d, NC)

        @pl.when(jnp.logical_not(is_self(dst)))
        def _():
            ab_copy(dst, slot, slot).wait_send()
            sums_copy(dst, slot, slot).wait_send()

    @pl.loop(1, NP)
    def _(d):
        group_copy(d, path).wait_send()


def output_stage(sums, ab, info, embed):
    vmem = pl.BlockSpec(memory_space=pltpu.VMEM)
    width = D // NP
    shape = jax.ShapeDtypeStruct((TB, width), F32)
    return pl.pallas_call(
        output_kernel,
        name="output_stage",
        out_shape=(shape, shape),
        in_specs=[vmem, vmem, vmem, pl.BlockSpec(memory_space=pl.ANY)],
        out_specs=(vmem, vmem),
        scratch_shapes=[
            pltpu.VMEM((NC, CH, TB), BF16),
            pltpu.VMEM((NC, 8, TB), F32),
            pltpu.VMEM((NP, 8, TB), F32),
            pltpu.VMEM((8, TB), F32),
            pltpu.VMEM((VOCAB, width), BF16),
            pltpu.VMEM((TB, width), F32),
            pltpu.VMEM((TB, width), F32),
            pltpu.SemaphoreType.DMA((NC,)),
            pltpu.SemaphoreType.DMA((NC,)),
            pltpu.SemaphoreType.DMA((NC,)),
            pltpu.SemaphoreType.DMA((NC,)),
            pltpu.SemaphoreType.DMA((NP,)),
            pltpu.SemaphoreType.DMA((NP,)),
            pltpu.SemaphoreType.DMA((3,)),
        ],
        compiler_params=pltpu.CompilerParams(
            collective_id=1, has_side_effects=True, vmem_limit_bytes=VMEM_LIMIT
        ),
    )(sums, ab, info, embed)


def body(tokens, sub_pos, sub_base, embed, norm_gain, fir_taps, long_filter, skip_gain, cotangent):
    info, cols = gather_stage(tokens, sub_pos, sub_base, embed, cotangent)
    sums, ab = channel_stage(info, cols, embed, norm_gain, fir_taps, long_filter, skip_gain)
    return output_stage(sums, ab, info, embed)


def solution(mesh):
    return jax.shard_map(
        body,
        mesh=mesh,
        in_specs=(
            P("ctx"),
            P("ctx"),
            P("ctx"),
            P(),
            P(),
            P(),
            P(None, "ctx"),
            P("ctx"),
            P("ctx", None),
        ),
        out_specs=(P("ctx", "path"), P("ctx", "path")),
        check_vma=False,
    )
```

```python
import functools

import jax
import jax.numpy as jnp
from jax import lax
from jax.experimental import pallas as pl
from jax.experimental.pallas import tpu as pltpu
from jax.sharding import PartitionSpec as P

MESH = pl.DeviceIdType.MESH
F32 = jnp.float32
BF16 = jnp.bfloat16

NP = 4
NC = 32
TB = 128
CH = 32
NB = 32
SUB = 16
VOCAB = 512
D = 4096
REACH = 2
STRIDE = CH + 1
UNROLL = 1
CHUNK = 4
ALPHAS = tuple((a + 0.5) / NP for a in range(NP))
VMEM_LIMIT = 60 * 1024 * 1024


def iota(shape, dim):
    return lax.broadcasted_iota(jnp.int32, shape, dim)


def rounded(x):
    return x.astype(BF16).astype(F32)


def nt_dot(a, b):
    return lax.dot_general(a, b, (((1,), (1,)), ((), ())), preferred_element_type=F32)


def gather_kernel(
    tok_ref,
    sub_pos_ref,
    sub_base_ref,
    embed_ref,
    cot_ref,
    info_ref,
    cols_ref,
    mine,
    parts,
    info_send,
    info_recv,
    cols_send,
    cols_recv,
    own_sem,
):
    path = lax.axis_index("path")
    me = lax.axis_index("ctx")

    barrier = pltpu.get_barrier_semaphore()

    @pl.loop(1, NC)
    def _(d):
        pl.semaphore_signal(
            barrier, inc=1, device_id={"ctx": lax.rem(me + d, NC)}, device_id_type=MESH
        )

    pick = (iota((CH, TB), 1) == iota((CH, TB), 0) + path * CH).astype(F32).astype(BF16)

    @pl.loop(0, NC)
    def _(j):
        block = cot_ref[:, pl.ds(pl.multiple_of(j * TB, TB), TB)]
        parts[j] = nt_dot(pick, block).astype(BF16)

    pl.semaphore_wait(barrier, NC - 1)

    def cols_copy(d, dst, slot):
        return pltpu.make_async_remote_copy(
            src_ref=parts.at[dst],
            dst_ref=cols_ref.at[slot],
            send_sem=cols_send.at[d],
            recv_sem=cols_recv.at[d],
            device_id={"ctx": dst},
            device_id_type=MESH,
        )

    def info_copy(d, dst, slot):
        return pltpu.make_async_remote_copy(
            src_ref=mine,
            dst_ref=info_ref.at[slot],
            send_sem=info_send.at[d],
            recv_sem=info_recv.at[d],
            device_id={"ctx": dst},
            device_id_type=MESH,
        )

    @pl.loop(1, NC)
    def _(d):
        cols_copy(d, lax.rem(me + d, NC), me).start()

    own_cols = pltpu.make_async_copy(parts.at[me], cols_ref.at[me], own_sem.at[0])
    own_cols.start()

    tok = tok_ref[...].astype(F32)
    diag = iota((SUB, SUB), 0) == iota((SUB, SUB), 1)
    pos_row = (sub_pos_ref[...] & 7).astype(F32)
    pos_col = jnp.sum(jnp.where(diag, pos_row, 0.0), 1, keepdims=True) + 8.0 * iota(
        (SUB, 1), 0
    ).astype(F32)
    base_col = jnp.sum(jnp.where(diag, sub_base_ref[...].astype(F32), 0.0), 1, keepdims=True)
    at_sub = iota((SUB, TB), 1).astype(F32) == pos_col
    covered = jnp.sum(jnp.where(at_sub, 1.0, 0.0), 0, keepdims=True) > 0.5
    base = jnp.where(
        covered, jnp.sum(jnp.where(at_sub, base_col, 0.0), 0, keepdims=True), tok
    )
    sub_tok_col = jnp.sum(jnp.where(at_sub, tok, 0.0), 1, keepdims=True)
    eye = iota((TB, TB), 0) == iota((TB, TB), 1)
    tok_col = jnp.sum(jnp.where(eye, tok, 0.0), 1, keepdims=True)
    ids = jnp.concatenate([tok_col, sub_tok_col, base_col], 0)
    rows = TB + 2 * SUB
    hot = (iota((rows, VOCAB), 1).astype(F32) == ids).astype(F32).astype(BF16)

    def squares(step, carry):
        plain, subs = carry
        part = embed_ref[:, pl.ds(pl.multiple_of(step * 256, 256), 256)]
        found = jnp.dot(hot, part, preferred_element_type=F32)
        own = found[:TB]
        own = own * own
        plain = plain + own[:, :TB] + own[:, TB:]
        e_tok = found[TB : TB + SUB]
        e_base = found[TB + SUB :]
        diff = e_tok - e_base
        new = []
        for a in range(NP):
            x = e_base + ALPHAS[a] * diff
            x = x * x
            new.append(subs[a] + x[:, :TB] + x[:, TB:])
        return plain, tuple(new)

    plain, subs = lax.fori_loop(
        0,
        D // 256,
        squares,
        (jnp.zeros((TB, TB), F32), tuple(jnp.zeros((SUB, TB), F32) for _ in range(NP))),
    )

    def inverse(total):
        return lax.rsqrt(jnp.sum(total, 1, keepdims=True) / D + 1e-06)

    plain_row = jnp.sum(jnp.where(eye, inverse(plain), 0.0), 0, keepdims=True)
    for a in range(NP):
        sub_row = jnp.sum(jnp.where(at_sub, inverse(subs[a]), 0.0), 0, keepdims=True)
        mine[a : a + 1, :] = jnp.where(covered, sub_row, plain_row)
    mine[4:5, :] = tok
    mine[5:6, :] = base
    mine[6:8, :] = jnp.zeros((2, TB), F32)

    @pl.loop(1, NC)
    def _(d):
        info_copy(d, lax.rem(me + d, NC), me).start()

    own_info = pltpu.make_async_copy(mine, info_ref.at[me], own_sem.at[1])
    own_info.start()

    @pl.loop(1, NC)
    def _(d):
        dst = lax.rem(me + d, NC)
        src = lax.rem(me - d + NC, NC)
        cols_copy(d, dst, src).wait_recv()
        info_copy(d, dst, src).wait_recv()
        cols_copy(d, dst, me).wait_send()
        info_copy(d, dst, me).wait_send()

    own_cols.wait()
    own_info.wait()


def gather_stage(tokens, sub_pos, sub_base, embed, cotangent):
    vmem = pl.BlockSpec(memory_space=pltpu.VMEM)
    return pl.pallas_call(
        gather_kernel,
        name="gather_stage",
        out_shape=(
            jax.ShapeDtypeStruct((NC, 8, TB), F32),
            jax.ShapeDtypeStruct((NC, CH, TB), BF16),
        ),
        in_specs=[vmem] * 5,
        out_specs=(vmem, vmem),
        scratch_shapes=[
            pltpu.VMEM((8, TB), F32),
            pltpu.VMEM((NC, CH, TB), BF16),
            pltpu.SemaphoreType.DMA((NC,)),
            pltpu.SemaphoreType.DMA((NC,)),
            pltpu.SemaphoreType.DMA((NC,)),
            pltpu.SemaphoreType.DMA((NC,)),
            pltpu.SemaphoreType.DMA((2,)),
        ],
        compiler_params=pltpu.CompilerParams(
            collective_id=0, has_side_effects=True, vmem_limit_bytes=VMEM_LIMIT
        ),
    )(tokens.reshape(1, -1), sub_pos.reshape(1, -1), sub_base.reshape(1, -1), embed, cotangent)


def take_lanes(table, index):
    rows = table.shape[0]
    low = jnp.broadcast_to(index & (TB - 1), (8, TB))
    high = jnp.broadcast_to(index >> 7, (8, TB))
    out = []
    for r in range(0, rows, 8):
        got = jnp.take_along_axis(table[r : r + 8, :TB], low, axis=1)
        for v in range(1, VOCAB // TB):
            more = jnp.take_along_axis(table[r : r + 8, v * TB : (v + 1) * TB], low, axis=1)
            got = jnp.where(high == v, more, got)
        out.append(got)
    return jnp.concatenate(out, 0)


def channel_kernel(
    path_index,
    ctx_index,
    info_ref,
    cols_ref,
    embed_ref,
    gain_ref,
    taps_ref,
    filter_ref,
    skip_ref,
    out_ref,
    ab_ref,
    emb_buf,
    table,
    taps,
    coef,
    time_filter,
    e_base_s,
    diff_s,
    key_s,
    val_s,
    stage,
    conv,
    past,
    ahead,
    sem,
):
    path = path_index()
    ctx = ctx_index()
    lanes = pl.ds(pl.multiple_of(ctx * TB, TB), TB)
    load = pltpu.make_async_copy(embed_ref.at[:, lanes], emb_buf, sem)
    load.start()

    lane = iota((CH, TB), 1)
    chosen = lane == iota((CH, TB), 0) + path * CH
    pick = chosen.astype(F32).astype(BF16)

    def column(row):
        return jnp.broadcast_to(
            jnp.sum(jnp.where(chosen, row, 0.0), 1, keepdims=True), (CH, TB)
        )

    coef[0] = column(gain_ref[pl.ds(ctx, 1), :])
    coef[1] = column(skip_ref[...])
    for f in range(3):
        for j in range(3):
            taps[f * 3 + j] = column(taps_ref[f, j : j + 1, lanes].astype(F32))

    @pl.loop(0, NB)
    def _(k):
        part = filter_ref[pl.ds(pl.multiple_of(k * TB, TB), TB), :].astype(BF16)
        time_filter[k] = nt_dot(pick, part)

    load.wait()
    table[...] = nt_dot(pick, emb_buf[...])

    flip = (iota((TB, TB), 0) + iota((TB, TB), 1) == TB - 1).astype(F32).astype(BF16)
    past[...] = jnp.zeros_like(past)

    def forward(a, _):
        info = info_ref[a]
        e_tok = take_lanes(table[...], info[4:5].astype(jnp.int32))
        e_base = take_lanes(table[...], info[5:6].astype(jnp.int32))
        diff = e_tok - e_base
        e_base_s[a] = e_base
        diff_s[a] = diff
        cot = cols_ref[a].astype(F32)
        gain = coef[0]
        grads = []
        for p in range(NP):
            now = rounded((e_base + ALPHAS[p] * diff) * info[p : p + 1] * gain)
            one = pltpu.roll(now, 1, 1)
            two = pltpu.roll(now, 2, 1)
            now1 = jnp.where(lane < 1, past[p, 0], one)
            now2 = jnp.where(lane < 2, past[p, 1], two)
            past[p, 0] = one
            past[p, 1] = two
            q, k, v = (
                taps[f * 3] * now + taps[f * 3 + 1] * now1 + taps[f * 3 + 2] * now2
                for f in range(3)
            )
            key_s[a, p] = k
            val_s[a, p] = v
            stage[a, p * STRIDE : p * STRIDE + CH, :] = rounded(k * v)
            grads.append((cot * q).astype(BF16))
        turned = jnp.dot(jnp.concatenate(grads, 0), flip, preferred_element_type=F32)
        for p in range(NP):
            at = (NP + p) * STRIDE
            stage[NB - 1 - a, at : at + CH, :] = turned[p * CH : (p + 1) * CH]
        return 0

    lax.fori_loop(0, NB, forward, 0)

    lane16 = iota((16, TB), 1)
    sub16 = iota((16, TB), 0)
    zero_tile = jnp.zeros((16, TB), BF16)

    def channel(c):
        rows = pl.ds(c, 8, stride=STRIDE)
        data = [
            jnp.concatenate([stage[2 * t, rows, :], stage[2 * t + 1, rows, :]], 0).astype(BF16)
            for t in range(NB // 2)
        ]
        before = jnp.zeros((16, TB), F32)
        rolled = [zero_tile] * 8
        blocks = []
        acc = None
        for k in range(NB):
            row = jnp.broadcast_to(time_filter[k, pl.ds(c, 1), :], (16, TB))
            turned = pltpu.roll(row, 0, 1, stride=1, stride_axis=0)
            shear = jnp.where(lane16 >= sub16, turned, before).astype(BF16)
            before = turned
            tiles = [shear]
            now = [shear]
            for g in range(1, TB // 16):
                moved = pltpu.roll(shear, 16 * g, 1)
                tiles.append(jnp.where(lane16 >= 16 * g, moved, rolled[g]))
                now.append(moved)
            rolled = now
            blocks.append(jnp.concatenate(tiles, 0))
            if k % (2 * CHUNK) == 2 * CHUNK - 1:
                first = k // 2 - CHUNK + 1
                rhs = jnp.concatenate(
                    [
                        jnp.concatenate([blocks[2 * n], blocks[2 * n + 1]], 1)
                        for n in range(CHUNK)
                    ],
                    0,
                )
                blocks = []
                lhs = jnp.concatenate(
                    [
                        jnp.concatenate([zero_tile] * n + data[: NB // 2 - n], 0)
                        for n in range(CHUNK)
                    ],
                    1,
                )
                size = 256 - 16 * first
                part = jnp.dot(lhs[:size], rhs, preferred_element_type=F32)
                if acc is None:
                    acc = part
                else:
                    acc = jnp.concatenate([acc[: 16 * first], acc[16 * first :] + part], 0)
        for a in range(NB):
            out = acc[8 * a : 8 * a + 8, :TB]
            if a > 0:
                out = out + acc[8 * a - 8 : 8 * a, TB:]
            conv[a, rows, :] = out

    def channels(step, _):
        for n in range(UNROLL):
            channel(step * UNROLL + n)
        return 0

    lax.fori_loop(0, CH // UNROLL, channels, 0)

    ahead[...] = jnp.zeros_like(ahead)

    def backward(step, _):
        a = NB - 1 - step
        info = info_ref[a]
        cot = cols_ref[a].astype(F32)
        e_base = e_base_s[a]
        diff = diff_s[a]
        gain = coef[0]
        skip = coef[1]
        turned = []
        for p in range(NP):
            rows = slice((NP + p) * STRIDE, (NP + p) * STRIDE + CH)
            turned.append(
                (conv[step, rows, :] + skip * stage[step, rows, :]).astype(BF16)
            )
        grad_z = jnp.dot(jnp.concatenate(turned, 0), flip, preferred_element_type=F32)
        total = jnp.zeros((CH, TB), F32)
        sum_a = jnp.zeros((CH, TB), F32)
        sum_b = jnp.zeros((CH, TB), F32)
        for p in range(NP):
            rows = slice(p * STRIDE, p * STRIDE + CH)
            out = rounded(conv[a, rows, :] + skip * stage[a, rows, :])
            gz = grad_z[p * CH : (p + 1) * CH]
            gq = rounded(cot * out)
            gk = rounded(gz * val_s[a, p])
            gv = rounded(gz * key_s[a, p])
            u0, u1, u2 = (taps[j] * gq + taps[3 + j] * gk + taps[6 + j] * gv for j in range(3))
            one = pltpu.roll(u1, TB - 1, 1)
            two = pltpu.roll(u2, TB - 2, 1)
            gn = (
                u0
                + jnp.where(lane < TB - 1, one, ahead[p, 0])
                + jnp.where(lane < TB - 2, two, ahead[p, 1])
            )
            ahead[p, 0] = one
            ahead[p, 1] = two
            inv = info[p : p + 1]
            scaled = gain * gn
            total = total + inv * scaled
            w = (e_base + ALPHAS[p] * diff) * scaled * (inv * inv * inv)
            sum_a = sum_a + w
            sum_b = sum_b + ALPHAS[p] * w
        out_ref[a] = total.astype(BF16)
        ab_ref[a, 0:1, :] = jnp.sum(sum_a, 0, keepdims=True)
        ab_ref[a, 1:2, :] = jnp.sum(sum_b, 0, keepdims=True)
        ab_ref[a, 2:8, :] = jnp.zeros((6, TB), F32)
        return 0

    lax.fori_loop(0, NB, backward, 0)


def axis_path():
    return lax.axis_index("path")


def axis_ctx():
    return lax.axis_index("ctx")


def channel_stage(
    info, cols, embed, gain, taps, long_filter, skip, path_index=axis_path, ctx_index=axis_ctx
):
    vmem = pl.BlockSpec(memory_space=pltpu.VMEM)
    return pl.pallas_call(
        functools.partial(channel_kernel, path_index, ctx_index),
        name="channel_stage",
        out_shape=(
            jax.ShapeDtypeStruct((NB, CH, TB), BF16),
            jax.ShapeDtypeStruct((NB, 8, TB), F32),
        ),
        in_specs=[vmem, vmem, pl.BlockSpec(memory_space=pl.ANY), vmem, vmem, vmem, vmem],
        out_specs=(vmem, vmem),
        scratch_shapes=[
            pltpu.VMEM((VOCAB, TB), BF16),
            pltpu.VMEM((CH, VOCAB), F32),
            pltpu.VMEM((9, CH, TB), F32),
            pltpu.VMEM((2, CH, TB), F32),
            pltpu.VMEM((NB, CH, TB), F32),
            pltpu.VMEM((NB, CH, TB), F32),
            pltpu.VMEM((NB, CH, TB), F32),
            pltpu.VMEM((NB, NP, CH, TB), F32),
            pltpu.VMEM((NB, NP, CH, TB), F32),
            pltpu.VMEM((NB, 2 * NP * STRIDE, TB), F32),
            pltpu.VMEM((NB, 2 * NP * STRIDE, TB), F32),
            pltpu.VMEM((NP, 2, CH, TB), F32),
            pltpu.VMEM((NP, 2, CH, TB), F32),
            pltpu.SemaphoreType.DMA,
        ],
        compiler_params=pltpu.CompilerParams(vmem_limit_bytes=VMEM_LIMIT),
    )(info, cols, embed, gain.reshape(-1, TB), taps, long_filter, skip.reshape(1, -1))


def output_kernel(
    sums_ref,
    ab_ref,
    info_ref,
    embed_ref,
    grad_ref,
    attr_ref,
    got,
    got_ab,
    group_ab,
    own_ab,
    emb_buf,
    base_s,
    diff_s,
    sums_send,
    sums_recv,
    ab_send,
    ab_recv,
    group_send,
    group_recv,
    own_sem,
):
    path = lax.axis_index("path")
    me = lax.axis_index("ctx")
    width = D // NP
    load = pltpu.make_async_copy(
        embed_ref.at[:, pl.ds(pl.multiple_of(path * width, width), width)], emb_buf, own_sem.at[2]
    )
    load.start()
    barrier = pltpu.get_barrier_semaphore()
    to_path = me // 8
    slot = (me % 8) * NP + path
    own = jnp.where(to_path == path, 1, 0)

    @pl.loop(0, NC)
    def _(s):
        src_path = lax.rem(s, NP)
        src_ctx = path * 8 + s // NP

        @pl.when((src_path != path) | (src_ctx != me))
        def _():
            pl.semaphore_signal(
                barrier,
                inc=1,
                device_id={"path": src_path, "ctx": src_ctx},
                device_id_type=MESH,
            )

    @pl.loop(1, NP)
    def _(d):
        pl.semaphore_signal(
            barrier, inc=1, device_id={"path": lax.rem(path + d, NP)}, device_id_type=MESH
        )

    pl.semaphore_wait(barrier, NC + NP - 1 - own)

    def sums_copy(dst, at, number):
        return pltpu.make_async_remote_copy(
            src_ref=sums_ref.at[dst],
            dst_ref=got.at[at],
            send_sem=sums_send.at[dst],
            recv_sem=sums_recv.at[number],
            device_id={"path": to_path, "ctx": dst},
            device_id_type=MESH,
        )

    def ab_copy(dst, at, number):
        return pltpu.make_async_remote_copy(
            src_ref=ab_ref.at[dst],
            dst_ref=got_ab.at[at],
            send_sem=ab_send.at[dst],
            recv_sem=ab_recv.at[number],
            device_id={"path": to_path, "ctx": dst},
            device_id_type=MESH,
        )

    def group_copy(d, at):
        return pltpu.make_async_remote_copy(
            src_ref=own_ab,
            dst_ref=group_ab.at[at],
            send_sem=group_send.at[d],
            recv_sem=group_recv.at[d],
            device_id={"path": lax.rem(path + d, NP)},
            device_id_type=MESH,
        )

    def is_self(dst):
        return (to_path == path) & (dst == me)

    own_sums = pltpu.make_async_copy(sums_ref.at[me], got.at[slot], own_sem.at[0])
    own_part = pltpu.make_async_copy(ab_ref.at[me], got_ab.at[slot], own_sem.at[1])

    @pl.when(to_path == path)
    def _():
        own_sums.start()
        own_part.start()

    @pl.loop(0, NC)
    def _(d):
        dst = lax.rem(me + d, NC)

        @pl.when(jnp.logical_not(is_self(dst)))
        def _():
            ab_copy(dst, slot, slot).start()
            sums_copy(dst, slot, slot).start()

    load.wait()
    info = info_ref[pl.ds(me, 1)][0]
    eye = iota((TB, TB), 0) == iota((TB, TB), 1)
    unit = eye.astype(F32).astype(BF16)

    def as_column(row):
        return jnp.sum(jnp.where(eye, row, 0.0), 1, keepdims=True)

    vocab = iota((TB, VOCAB), 1).astype(F32)
    hot_tok = (vocab == as_column(info[4:5])).astype(F32).astype(BF16)
    hot_base = (vocab == as_column(info[5:6])).astype(F32).astype(BF16)

    @pl.loop(0, width // 256)
    def _(s):
        columns = pl.ds(pl.multiple_of(s * 256, 256), 256)
        part = emb_buf[:, columns]
        e_tok = jnp.dot(hot_tok, part, preferred_element_type=F32)
        e_base = jnp.dot(hot_base, part, preferred_element_type=F32)
        base_s[:, columns] = e_base
        diff_s[:, columns] = e_tok - e_base

    self_slot = (me % 8) * NP + path

    def others(s):
        return jnp.logical_not((to_path == path) & (s == self_slot))

    @pl.loop(0, NC)
    def _(s):
        @pl.when(others(s))
        def _():
            ab_copy(me, s, s).wait_recv()

    @pl.when(to_path == path)
    def _():
        own_part.wait()

    own_ab[...] = jnp.sum(got_ab[...], 0)

    @pl.loop(1, NP)
    def _(d):
        group_copy(d, path).start()

    @pl.loop(0, NC)
    def _(s):
        @pl.when(others(s))
        def _():
            sums_copy(me, s, s).wait_recv()

    @pl.when(to_path == path)
    def _():
        own_sums.wait()

    ab = own_ab[...]
    for d in range(1, NP):
        src = lax.rem(path - d + NP, NP)
        group_copy(d, src).wait_recv()
        ab = ab + group_ab[pl.ds(src, 1)][0]
    scale = 1.0 / (NP * D)
    a_col = as_column(ab[0:1]) * scale
    b_col = as_column(ab[1:2]) * scale

    @pl.loop(0, width // TB)
    def _(s):
        columns = pl.ds(pl.multiple_of(s * TB, TB), TB)
        block = got[pl.ds(s * 4, 4)].reshape(TB, TB)
        summed = nt_dot(unit, block)
        diff = diff_s[:, columns]
        grad = summed * (1.0 / NP) - (base_s[:, columns] * a_col + diff * b_col)
        grad_ref[:, columns] = grad
        attr_ref[:, columns] = diff * grad

    @pl.loop(0, NC)
    def _(d):
        dst = lax.rem(me + d, NC)

        @pl.when(jnp.logical_not(is_self(dst)))
        def _():
            ab_copy(dst, slot, slot).wait_send()
            sums_copy(dst, slot, slot).wait_send()

    @pl.loop(1, NP)
    def _(d):
        group_copy(d, path).wait_send()


def output_stage(sums, ab, info, embed):
    vmem = pl.BlockSpec(memory_space=pltpu.VMEM)
    width = D // NP
    shape = jax.ShapeDtypeStruct((TB, width), F32)
    return pl.pallas_call(
        output_kernel,
        name="output_stage",
        out_shape=(shape, shape),
        in_specs=[vmem, vmem, vmem, pl.BlockSpec(memory_space=pl.ANY)],
        out_specs=(vmem, vmem),
        scratch_shapes=[
            pltpu.VMEM((NC, CH, TB), BF16),
            pltpu.VMEM((NC, 8, TB), F32),
            pltpu.VMEM((NP, 8, TB), F32),
            pltpu.VMEM((8, TB), F32),
            pltpu.VMEM((VOCAB, width), BF16),
            pltpu.VMEM((TB, width), F32),
            pltpu.VMEM((TB, width), F32),
            pltpu.SemaphoreType.DMA((NC,)),
            pltpu.SemaphoreType.DMA((NC,)),
            pltpu.SemaphoreType.DMA((NC,)),
            pltpu.SemaphoreType.DMA((NC,)),
            pltpu.SemaphoreType.DMA((NP,)),
            pltpu.SemaphoreType.DMA((NP,)),
            pltpu.SemaphoreType.DMA((3,)),
        ],
        compiler_params=pltpu.CompilerParams(
            collective_id=1, has_side_effects=True, vmem_limit_bytes=VMEM_LIMIT
        ),
    )(sums, ab, info, embed)


def body(tokens, sub_pos, sub_base, embed, norm_gain, fir_taps, long_filter, skip_gain, cotangent):
    info, cols = gather_stage(tokens, sub_pos, sub_base, embed, cotangent)
    sums, ab = channel_stage(info, cols, embed, norm_gain, fir_taps, long_filter, skip_gain)
    return output_stage(sums, ab, info, embed)


def solution(mesh):
    return jax.shard_map(
        body,
        mesh=mesh,
        in_specs=(
            P("ctx"),
            P("ctx"),
            P("ctx"),
            P(),
            P(),
            P(),
            P(None, "ctx"),
            P("ctx"),
            P("ctx", None),
        ),
        out_specs=(P("ctx", "path"), P("ctx", "path")),
        check_vma=False,
    )
```

```python
import jax
import jax.numpy as jnp
from jax import lax
from jax.experimental import pallas as pl
from jax.experimental.pallas import tpu as pltpu
from jax.sharding import PartitionSpec as P

MESH = pl.DeviceIdType.MESH
F32 = jnp.float32
BF16 = jnp.bfloat16

NP = 4
NC = 32
TB = 128
CH = 32
NB = 32
SUB = 16
VOCAB = 512
D = 4096
REACH = 2
STRIDE = CH + 1
UNROLL = 1
CHUNK = 4
ALPHAS = tuple((a + 0.5) / NP for a in range(NP))
VMEM_LIMIT = 60 * 1024 * 1024


def iota(shape, dim):
    return lax.broadcasted_iota(jnp.int32, shape, dim)


def rounded(x):
    return x.astype(BF16).astype(F32)


def nt_dot(a, b):
    return lax.dot_general(a, b, (((1,), (1,)), ((), ())), preferred_element_type=F32)


def take_lanes(table, index):
    rows = table.shape[0]
    low = jnp.broadcast_to(index & (TB - 1), (8, TB))
    high = jnp.broadcast_to(index >> 7, (8, TB))
    out = []
    for r in range(0, rows, 8):
        got = jnp.take_along_axis(table[r : r + 8, :TB], low, axis=1)
        for v in range(1, VOCAB // TB):
            more = jnp.take_along_axis(table[r : r + 8, v * TB : (v + 1) * TB], low, axis=1)
            got = jnp.where(high == v, more, got)
        out.append(got)
    return jnp.concatenate(out, 0)


def fused_kernel(
    tok_ref,
    sub_pos_ref,
    sub_base_ref,
    embed_hbm,
    gain_ref,
    taps_ref,
    filter_hbm,
    skip_ref,
    cot_hbm,
    grad_ref,
    attr_ref,
    embed_ref,
    filter_ref,
    cot_ref,
    mine,
    parts,
    info_ref,
    cols_ref,
    table,
    taps,
    coef,
    time_filter,
    e_base_s,
    diff_s,
    key_s,
    val_s,
    stage,
    conv,
    past,
    ahead,
    sums,
    ab,
    got,
    got_ab,
    own_ab,
    group_ab,
    out_base,
    out_diff,
    load_sem,
    info_send,
    info_recv,
    cols_send,
    cols_recv,
    sums_send,
    sums_recv,
    ab_send,
    ab_recv,
    group_send,
    group_recv,
):
    path = lax.axis_index("path")
    me = lax.axis_index("ctx")
    width = D // NP
    to_path = me // 8
    slot = (me % 8) * NP + path
    own = jnp.where(to_path == path, 1, 0)

    load_cot = pltpu.make_async_copy(cot_hbm, cot_ref, load_sem.at[0])
    load_embed = pltpu.make_async_copy(embed_hbm, embed_ref, load_sem.at[1])
    load_filter = pltpu.make_async_copy(filter_hbm, filter_ref, load_sem.at[2])
    load_cot.start()
    load_embed.start()
    load_filter.start()

    barrier = pltpu.get_barrier_semaphore()

    @pl.loop(1, NC)
    def _(d):
        pl.semaphore_signal(
            barrier, inc=1, device_id={"ctx": lax.rem(me + d, NC)}, device_id_type=MESH
        )

    @pl.loop(0, NC)
    def _(s):
        src_path = lax.rem(s, NP)
        src_ctx = path * 8 + s // NP

        @pl.when((src_path != path) | (src_ctx != me))
        def _():
            pl.semaphore_signal(
                barrier,
                inc=1,
                device_id={"path": src_path, "ctx": src_ctx},
                device_id_type=MESH,
            )

    @pl.loop(1, NP)
    def _(d):
        pl.semaphore_signal(
            barrier, inc=1, device_id={"path": lax.rem(path + d, NP)}, device_id_type=MESH
        )

    def cols_copy(d, dst, at):
        return pltpu.make_async_remote_copy(
            src_ref=parts.at[dst],
            dst_ref=cols_ref.at[at],
            send_sem=cols_send.at[d],
            recv_sem=cols_recv.at[d],
            device_id={"ctx": dst},
            device_id_type=MESH,
        )

    def info_copy(d, dst, at):
        return pltpu.make_async_remote_copy(
            src_ref=mine,
            dst_ref=info_ref.at[at],
            send_sem=info_send.at[d],
            recv_sem=info_recv.at[d],
            device_id={"ctx": dst},
            device_id_type=MESH,
        )

    def sums_copy(dst, at, number):
        return pltpu.make_async_remote_copy(
            src_ref=sums.at[dst],
            dst_ref=got.at[at],
            send_sem=sums_send.at[dst],
            recv_sem=sums_recv.at[number],
            device_id={"path": to_path, "ctx": dst},
            device_id_type=MESH,
        )

    def ab_copy(dst, at, number):
        return pltpu.make_async_remote_copy(
            src_ref=ab.at[dst],
            dst_ref=got_ab.at[at],
            send_sem=ab_send.at[dst],
            recv_sem=ab_recv.at[number],
            device_id={"path": to_path, "ctx": dst},
            device_id_type=MESH,
        )

    def group_copy(d, at):
        return pltpu.make_async_remote_copy(
            src_ref=own_ab,
            dst_ref=group_ab.at[at],
            send_sem=group_send.at[d],
            recv_sem=group_recv.at[d],
            device_id={"path": lax.rem(path + d, NP)},
            device_id_type=MESH,
        )

    lane = iota((CH, TB), 1)
    chosen = lane == iota((CH, TB), 0) + path * CH
    pick = chosen.astype(F32).astype(BF16)
    load_cot.wait()

    @pl.loop(0, NC)
    def _(j):
        block = cot_ref[:, pl.ds(pl.multiple_of(j * TB, TB), TB)]
        parts[j] = nt_dot(pick, block).astype(BF16)

    cols_ref[pl.ds(me, 1)] = parts[pl.ds(me, 1)]

    tok = tok_ref[...].astype(F32)
    diag = iota((SUB, SUB), 0) == iota((SUB, SUB), 1)
    pos_row = (sub_pos_ref[...] & 7).astype(F32)
    pos_col = jnp.sum(jnp.where(diag, pos_row, 0.0), 1, keepdims=True) + 8.0 * iota(
        (SUB, 1), 0
    ).astype(F32)
    base_col = jnp.sum(jnp.where(diag, sub_base_ref[...].astype(F32), 0.0), 1, keepdims=True)
    at_sub = iota((SUB, TB), 1).astype(F32) == pos_col
    covered = jnp.sum(jnp.where(at_sub, 1.0, 0.0), 0, keepdims=True) > 0.5
    base = jnp.where(covered, jnp.sum(jnp.where(at_sub, base_col, 0.0), 0, keepdims=True), tok)
    sub_tok_col = jnp.sum(jnp.where(at_sub, tok, 0.0), 1, keepdims=True)
    eye = iota((TB, TB), 0) == iota((TB, TB), 1)

    def as_column(row):
        return jnp.sum(jnp.where(eye, row, 0.0), 1, keepdims=True)

    tok_col = as_column(tok)
    ids = jnp.concatenate([tok_col, sub_tok_col, base_col], 0)
    hot = (iota((TB + 2 * SUB, VOCAB), 1).astype(F32) == ids).astype(F32).astype(BF16)
    load_embed.wait()

    def squares(step, carry):
        plain, subs = carry
        part = embed_ref[:, pl.ds(pl.multiple_of(step * 256, 256), 256)]
        found = jnp.dot(hot, part, preferred_element_type=F32)
        plain_rows = found[:TB]
        plain_rows = plain_rows * plain_rows
        plain = plain + plain_rows[:, :TB] + plain_rows[:, TB:]
        e_tok = found[TB : TB + SUB]
        e_base = found[TB + SUB :]
        diff = e_tok - e_base
        new = []
        for a in range(NP):
            x = e_base + ALPHAS[a] * diff
            x = x * x
            new.append(subs[a] + x[:, :TB] + x[:, TB:])
        return plain, tuple(new)

    plain, subs = lax.fori_loop(
        0,
        D // 256,
        squares,
        (jnp.zeros((TB, TB), F32), tuple(jnp.zeros((SUB, TB), F32) for _ in range(NP))),
    )

    def inverse(total):
        return lax.rsqrt(jnp.sum(total, 1, keepdims=True) / D + 1e-06)

    plain_row = jnp.sum(jnp.where(eye, inverse(plain), 0.0), 0, keepdims=True)
    for a in range(NP):
        sub_row = jnp.sum(jnp.where(at_sub, inverse(subs[a]), 0.0), 0, keepdims=True)
        mine[a : a + 1, :] = jnp.where(covered, sub_row, plain_row)
    mine[4:5, :] = tok
    mine[5:6, :] = base
    mine[6:8, :] = jnp.zeros((2, TB), F32)
    info_ref[pl.ds(me, 1)] = mine[...].reshape(1, 8, TB)

    pl.semaphore_wait(barrier, 2 * NC + NP - 2 - own)

    @pl.loop(1, NC)
    def _(d):
        info_copy(d, lax.rem(me + d, NC), me).start()
        cols_copy(d, lax.rem(me + d, NC), me).start()

    lanes = pl.ds(pl.multiple_of(me * TB, TB), TB)

    def column(row):
        return jnp.broadcast_to(
            jnp.sum(jnp.where(chosen, row, 0.0), 1, keepdims=True), (CH, TB)
        )

    coef[0] = column(gain_ref[pl.ds(me, 1), :])
    coef[1] = column(skip_ref[...])
    for f in range(3):
        for j in range(3):
            taps[f * 3 + j] = column(taps_ref[f, j : j + 1, lanes].astype(F32))
    table[...] = nt_dot(pick, embed_ref[:, lanes])
    load_filter.wait()

    @pl.loop(0, NB)
    def _(k):
        part = filter_ref[pl.ds(pl.multiple_of(k * TB, TB), TB), :].astype(BF16)
        time_filter[k] = nt_dot(pick, part)

    vocab = iota((TB, VOCAB), 1).astype(F32)
    hot_tok = (vocab == tok_col).astype(F32).astype(BF16)
    hot_base = (vocab == as_column(base)).astype(F32).astype(BF16)

    @pl.loop(0, width // 256)
    def _(s):
        columns = pl.ds(pl.multiple_of(s * 256, 256), 256)
        part = embed_ref[:, pl.ds(pl.multiple_of(path * width + s * 256, 256), 256)]
        e_tok = jnp.dot(hot_tok, part, preferred_element_type=F32)
        e_base = jnp.dot(hot_base, part, preferred_element_type=F32)
        out_base[:, columns] = e_base
        out_diff[:, columns] = e_tok - e_base

    @pl.loop(1, NC)
    def _(d):
        dst = lax.rem(me + d, NC)
        src = lax.rem(me - d + NC, NC)
        info_copy(d, dst, src).wait_recv()
        cols_copy(d, dst, src).wait_recv()

    flip = (iota((TB, TB), 0) + iota((TB, TB), 1) == TB - 1).astype(F32).astype(BF16)
    past[...] = jnp.zeros_like(past)

    def forward(a, _):
        info = info_ref[a]
        e_tok = take_lanes(table[...], info[4:5].astype(jnp.int32))
        e_base = take_lanes(table[...], info[5:6].astype(jnp.int32))
        diff = e_tok - e_base
        e_base_s[a] = e_base
        diff_s[a] = diff
        cot = cols_ref[a].astype(F32)
        gain = coef[0]
        grads = []
        for p in range(NP):
            now = rounded((e_base + ALPHAS[p] * diff) * info[p : p + 1] * gain)
            one = pltpu.roll(now, 1, 1)
            two = pltpu.roll(now, 2, 1)
            now1 = jnp.where(lane < 1, past[p, 0], one)
            now2 = jnp.where(lane < 2, past[p, 1], two)
            past[p, 0] = one
            past[p, 1] = two
            q, k, v = (
                taps[f * 3] * now + taps[f * 3 + 1] * now1 + taps[f * 3 + 2] * now2
                for f in range(3)
            )
            key_s[a, p] = k
            val_s[a, p] = v
            stage[a, p * STRIDE : p * STRIDE + CH, :] = rounded(k * v)
            grads.append((cot * q).astype(BF16))
        turned = jnp.dot(jnp.concatenate(grads, 0), flip, preferred_element_type=F32)
        for p in range(NP):
            at = (NP + p) * STRIDE
            stage[NB - 1 - a, at : at + CH, :] = turned[p * CH : (p + 1) * CH]
        return 0

    lax.fori_loop(0, NB, forward, 0)

    lane16 = iota((16, TB), 1)
    sub16 = iota((16, TB), 0)
    zero_tile = jnp.zeros((16, TB), BF16)

    def channel(c):
        rows = pl.ds(c, 8, stride=STRIDE)
        data = [
            jnp.concatenate([stage[2 * t, rows, :], stage[2 * t + 1, rows, :]], 0).astype(BF16)
            for t in range(NB // 2)
        ]
        before = jnp.zeros((16, TB), F32)
        rolled = [zero_tile] * 8
        blocks = []
        acc = None
        for k in range(NB):
            row = jnp.broadcast_to(time_filter[k, pl.ds(c, 1), :], (16, TB))
            turned = pltpu.roll(row, 0, 1, stride=1, stride_axis=0)
            shear = jnp.where(lane16 >= sub16, turned, before).astype(BF16)
            before = turned
            tiles = [shear]
            now = [shear]
            for g in range(1, TB // 16):
                moved = pltpu.roll(shear, 16 * g, 1)
                tiles.append(jnp.where(lane16 >= 16 * g, moved, rolled[g]))
                now.append(moved)
            rolled = now
            blocks.append(jnp.concatenate(tiles, 0))
            if k % (2 * CHUNK) == 2 * CHUNK - 1:
                first = k // 2 - CHUNK + 1
                rhs = jnp.concatenate(
                    [
                        jnp.concatenate([blocks[2 * n], blocks[2 * n + 1]], 1)
                        for n in range(CHUNK)
                    ],
                    0,
                )
                blocks = []
                lhs = jnp.concatenate(
                    [
                        jnp.concatenate([zero_tile] * n + data[: NB // 2 - n], 0)
                        for n in range(CHUNK)
                    ],
                    1,
                )
                size = 256 - 16 * first
                part = jnp.dot(lhs[:size], rhs, preferred_element_type=F32)
                if acc is None:
                    acc = part
                else:
                    acc = jnp.concatenate([acc[: 16 * first], acc[16 * first :] + part], 0)
        for a in range(NB):
            out = acc[8 * a : 8 * a + 8, :TB]
            if a > 0:
                out = out + acc[8 * a - 8 : 8 * a, TB:]
            conv[a, rows, :] = out

    def channels(step, _):
        for n in range(UNROLL):
            channel(step * UNROLL + n)
        return 0

    lax.fori_loop(0, CH // UNROLL, channels, 0)

    ahead[...] = jnp.zeros_like(ahead)

    def is_self(dst):
        return (to_path == path) & (dst == me)

    def backward(step, _):
        a = lax.rem(me + 1 - step + 2 * NB, NB)
        info = info_ref[a]
        cot = cols_ref[a].astype(F32)
        e_base = e_base_s[a]
        diff = diff_s[a]
        gain = coef[0]
        skip = coef[1]
        turned = []
        for p in range(NP):
            rows = slice((NP + p) * STRIDE, (NP + p) * STRIDE + CH)
            turned.append(
                (conv[NB - 1 - a, rows, :] + skip * stage[NB - 1 - a, rows, :]).astype(BF16)
            )
        grad_z = jnp.dot(jnp.concatenate(turned, 0), flip, preferred_element_type=F32)
        total = jnp.zeros((CH, TB), F32)
        sum_a = jnp.zeros((CH, TB), F32)
        sum_b = jnp.zeros((CH, TB), F32)
        for p in range(NP):
            rows = slice(p * STRIDE, p * STRIDE + CH)
            out = rounded(conv[a, rows, :] + skip * stage[a, rows, :])
            gz = grad_z[p * CH : (p + 1) * CH]
            gq = rounded(cot * out)
            gk = rounded(gz * val_s[a, p])
            gv = rounded(gz * key_s[a, p])
            u0, u1, u2 = (taps[j] * gq + taps[3 + j] * gk + taps[6 + j] * gv for j in range(3))
            one = pltpu.roll(u1, TB - 1, 1)
            two = pltpu.roll(u2, TB - 2, 1)
            gn = (
                u0
                + jnp.where(lane < TB - 1, one, ahead[p, 0])
                + jnp.where(lane < TB - 2, two, ahead[p, 1])
            )
            ahead[p, 0] = one
            ahead[p, 1] = two
            inv = info[p : p + 1]
            scaled = gain * gn
            total = total + inv * scaled
            w = (e_base + ALPHAS[p] * diff) * scaled * (inv * inv * inv)
            sum_a = sum_a + w
            sum_b = sum_b + ALPHAS[p] * w

        @pl.when(step > 0)
        def _():
            sums[a] = total.astype(BF16)
            ab[a, 0:1, :] = jnp.sum(sum_a, 0, keepdims=True)
            ab[a, 1:2, :] = jnp.sum(sum_b, 0, keepdims=True)

            @pl.when(jnp.logical_not(is_self(a)))
            def _():
                ab_copy(a, slot, slot).start()
                sums_copy(a, slot, slot).start()

            @pl.when(is_self(a))
            def _():
                got[pl.ds(slot, 1)] = sums[pl.ds(a, 1)]
                got_ab[pl.ds(slot, 1)] = ab[pl.ds(a, 1)]

        @pl.when(a == 0)
        def _():
            ahead[...] = jnp.zeros_like(ahead)

        return 0

    lax.fori_loop(0, NB + 1, backward, 0)

    def others(s):
        return jnp.logical_not((to_path == path) & (s == slot))

    @pl.loop(0, NC)
    def _(s):
        @pl.when(others(s))
        def _():
            ab_copy(me, s, s).wait_recv()

    own_ab[...] = jnp.sum(got_ab[...], 0)

    @pl.loop(1, NP)
    def _(d):
        group_copy(d, path).start()

    @pl.loop(0, NC)
    def _(s):
        @pl.when(others(s))
        def _():
            sums_copy(me, s, s).wait_recv()

    both = own_ab[...]
    for d in range(1, NP):
        src = lax.rem(path - d + NP, NP)
        group_copy(d, src).wait_recv()
        both = both + group_ab[pl.ds(src, 1)][0]
    scale = 1.0 / (NP * D)
    a_col = as_column(both[0:1]) * scale
    b_col = as_column(both[1:2]) * scale
    unit = eye.astype(F32).astype(BF16)

    @pl.loop(0, width // TB)
    def _(s):
        columns = pl.ds(pl.multiple_of(s * TB, TB), TB)
        block = got[pl.ds(s * 4, 4)].reshape(TB, TB)
        summed = nt_dot(unit, block)
        diff = out_diff[:, columns]
        grad = summed * (1.0 / NP) - (out_base[:, columns] * a_col + diff * b_col)
        grad_ref[:, columns] = grad
        attr_ref[:, columns] = diff * grad

    @pl.loop(1, NC)
    def _(d):
        dst = lax.rem(me + d, NC)
        info_copy(d, dst, me).wait_send()
        cols_copy(d, dst, me).wait_send()

    @pl.loop(0, NC)
    def _(d):
        @pl.when(jnp.logical_not(is_self(d)))
        def _():
            ab_copy(d, slot, slot).wait_send()
            sums_copy(d, slot, slot).wait_send()

    @pl.loop(1, NP)
    def _(d):
        group_copy(d, path).wait_send()


def body(tokens, sub_pos, sub_base, embed, norm_gain, fir_taps, long_filter, skip_gain, cotangent):
    vmem = pl.BlockSpec(memory_space=pltpu.VMEM)
    here = pl.BlockSpec(memory_space=pl.ANY)
    width = D // NP
    shape = jax.ShapeDtypeStruct((TB, width), F32)
    dma = pltpu.SemaphoreType.DMA
    return pl.pallas_call(
        fused_kernel,
        name="fused_stage",
        out_shape=(shape, shape),
        in_specs=[vmem, vmem, vmem, here, vmem, vmem, here, vmem, here],
        out_specs=(vmem, vmem),
        scratch_shapes=[
            pltpu.VMEM((VOCAB, D), BF16),
            pltpu.VMEM((NB * TB, TB), F32),
            pltpu.VMEM((TB, D), BF16),
            pltpu.VMEM((8, TB), F32),
            pltpu.VMEM((NC, CH, TB), BF16),
            pltpu.VMEM((NC, 8, TB), F32),
            pltpu.VMEM((NC, CH, TB), BF16),
            pltpu.VMEM((CH, VOCAB), F32),
            pltpu.VMEM((9, CH, TB), F32),
            pltpu.VMEM((2, CH, TB), F32),
            pltpu.VMEM((NB, CH, TB), F32),
            pltpu.VMEM((NB, CH, TB), F32),
            pltpu.VMEM((NB, CH, TB), F32),
            pltpu.VMEM((NB, NP, CH, TB), F32),
            pltpu.VMEM((NB, NP, CH, TB), F32),
            pltpu.VMEM((NB, 2 * NP * STRIDE, TB), F32),
            pltpu.VMEM((NB, 2 * NP * STRIDE, TB), F32),
            pltpu.VMEM((NP, 2, CH, TB), F32),
            pltpu.VMEM((NP, 2, CH, TB), F32),
            pltpu.VMEM((NC, CH, TB), BF16),
            pltpu.VMEM((NC, 2, TB), F32),
            pltpu.VMEM((NC, CH, TB), BF16),
            pltpu.VMEM((NC, 2, TB), F32),
            pltpu.VMEM((2, TB), F32),
            pltpu.VMEM((NP, 2, TB), F32),
            pltpu.VMEM((TB, width), F32),
            pltpu.VMEM((TB, width), F32),
            dma((3,)),
            dma((NC,)),
            dma((NC,)),
            dma((NC,)),
            dma((NC,)),
            dma((NC,)),
            dma((NC,)),
            dma((NC,)),
            dma((NC,)),
            dma((NP,)),
            dma((NP,)),
        ],
        compiler_params=pltpu.CompilerParams(
            collective_id=0, has_side_effects=True, vmem_limit_bytes=VMEM_LIMIT
        ),
    )(
        tokens.reshape(1, -1),
        sub_pos.reshape(1, -1),
        sub_base.reshape(1, -1),
        embed,
        norm_gain.reshape(-1, TB),
        fir_taps,
        long_filter,
        skip_gain.reshape(1, -1),
        cotangent,
    )


def solution(mesh):
    return jax.shard_map(
        body,
        mesh=mesh,
        in_specs=(
            P("ctx"),
            P("ctx"),
            P("ctx"),
            P(),
            P(),
            P(),
            P(None, "ctx"),
            P("ctx"),
            P("ctx", None),
        ),
        out_specs=(P("ctx", "path"), P("ctx", "path")),
        check_vma=False,
    )
```

```python
import jax
import jax.numpy as jnp
from jax import lax
from jax.experimental import pallas as pl
from jax.experimental.pallas import tpu as pltpu
from jax.sharding import PartitionSpec as P

MESH = pl.DeviceIdType.MESH
F32 = jnp.float32
BF16 = jnp.bfloat16

NP = 4
NC = 32
TB = 128
CH = 32
NB = 32
SUB = 16
VOCAB = 512
D = 4096
REACH = 2
STRIDE = CH + 1
UNROLL = 1
CHUNK = 2
FLIPS = 4
OUT = 512
ALPHAS = tuple((a + 0.5) / NP for a in range(NP))
VMEM_LIMIT = 60 * 1024 * 1024


def iota(shape, dim):
    return lax.broadcasted_iota(jnp.int32, shape, dim)


def rounded(x):
    return x.astype(BF16).astype(F32)


def nt_dot(a, b):
    return lax.dot_general(a, b, (((1,), (1,)), ((), ())), preferred_element_type=F32)


def take_lanes(table, index):
    rows = table.shape[0]
    low = jnp.broadcast_to(index & (TB - 1), (8, TB))
    high = jnp.broadcast_to(index >> 7, (8, TB))
    out = []
    for r in range(0, rows, 8):
        got = jnp.take_along_axis(table[r : r + 8, :TB], low, axis=1)
        for v in range(1, VOCAB // TB):
            more = jnp.take_along_axis(table[r : r + 8, v * TB : (v + 1) * TB], low, axis=1)
            got = jnp.where(high == v, more, got)
        out.append(got)
    return jnp.concatenate(out, 0)


def fused_kernel(
    tok_ref,
    sub_pos_ref,
    sub_base_ref,
    embed_hbm,
    gain_ref,
    taps_ref,
    filter_hbm,
    skip_ref,
    cot_hbm,
    sums_out,
    both_out,
    tok_out,
    base_out,
    embed_ref,
    filter_ref,
    cot_ref,
    mine,
    parts,
    info_ref,
    cols_ref,
    table,
    taps,
    coef,
    time_filter,
    e_base_s,
    diff_s,
    key_s,
    val_s,
    stage,
    conv,
    past,
    ahead,
    sums,
    ab,
    got,
    got_ab,
    own_ab,
    group_ab,
    turn,
    grad_z,
    load_sem,
    info_send,
    info_recv,
    cols_send,
    cols_recv,
    sums_send,
    sums_recv,
    ab_send,
    ab_recv,
    group_send,
    group_recv,
):
    path = lax.axis_index("path")
    me = lax.axis_index("ctx")
    width = D // NP
    to_path = me // 8
    slot = (me % 8) * NP + path
    own = jnp.where(to_path == path, 1, 0)

    def partner(ctx):
        return jnp.where(ctx // 4 % 2 == me // 4 % 2, path, lax.rem(path + 2, NP))

    load_cot = pltpu.make_async_copy(cot_hbm, cot_ref, load_sem.at[0])
    load_embed = pltpu.make_async_copy(embed_hbm, embed_ref, load_sem.at[1])
    load_filter = pltpu.make_async_copy(filter_hbm, filter_ref, load_sem.at[2])
    load_cot.start()
    load_embed.start()
    load_filter.start()

    barrier = pltpu.get_barrier_semaphore()

    @pl.loop(1, NC)
    def _(d):
        other = lax.rem(me + d, NC)
        pl.semaphore_signal(
            barrier,
            inc=1,
            device_id={"path": partner(other), "ctx": other},
            device_id_type=MESH,
        )

    @pl.loop(0, NC)
    def _(s):
        src_path = lax.rem(s, NP)
        src_ctx = path * 8 + s // NP

        @pl.when((src_path != path) | (src_ctx != me))
        def _():
            pl.semaphore_signal(
                barrier,
                inc=1,
                device_id={"path": src_path, "ctx": src_ctx},
                device_id_type=MESH,
            )

    @pl.loop(1, NP)
    def _(d):
        pl.semaphore_signal(
            barrier, inc=1, device_id={"path": lax.rem(path + d, NP)}, device_id_type=MESH
        )

    def cols_copy(d, dst, at):
        return pltpu.make_async_remote_copy(
            src_ref=parts.at[dst],
            dst_ref=cols_ref.at[at],
            send_sem=cols_send.at[d],
            recv_sem=cols_recv.at[d],
            device_id={"path": partner(dst), "ctx": dst},
            device_id_type=MESH,
        )

    def info_copy(d, dst, at):
        return pltpu.make_async_remote_copy(
            src_ref=mine,
            dst_ref=info_ref.at[at],
            send_sem=info_send.at[d],
            recv_sem=info_recv.at[d],
            device_id={"path": partner(dst), "ctx": dst},
            device_id_type=MESH,
        )

    def sums_copy(dst, at, number):
        return pltpu.make_async_remote_copy(
            src_ref=sums.at[dst],
            dst_ref=got.at[at],
            send_sem=sums_send.at[dst],
            recv_sem=sums_recv.at[number],
            device_id={"path": to_path, "ctx": dst},
            device_id_type=MESH,
        )

    def ab_copy(dst, at, number):
        return pltpu.make_async_remote_copy(
            src_ref=ab.at[dst],
            dst_ref=got_ab.at[at],
            send_sem=ab_send.at[dst],
            recv_sem=ab_recv.at[number],
            device_id={"path": to_path, "ctx": dst},
            device_id_type=MESH,
        )

    def group_copy(d, at):
        return pltpu.make_async_remote_copy(
            src_ref=own_ab,
            dst_ref=group_ab.at[at],
            send_sem=group_send.at[d],
            recv_sem=group_recv.at[d],
            device_id={"path": lax.rem(path + d, NP)},
            device_id_type=MESH,
        )

    lane = iota((CH, TB), 1)
    chosen = lane == iota((CH, TB), 0) + path * CH
    pick = chosen.astype(F32).astype(BF16)
    load_cot.wait()

    @pl.loop(0, NC // 4)
    def _(step):
        to = partner(4 * step)
        want = (lane == iota((CH, TB), 0) + to * CH).astype(F32).astype(BF16)
        for n in range(4):
            block = cot_ref[:, pl.ds(pl.multiple_of((4 * step + n) * TB, TB), TB)]
            parts[4 * step + n] = nt_dot(want, block).astype(BF16)

    cols_ref[pl.ds(me, 1)] = parts[pl.ds(me, 1)]

    tok = tok_ref[...].astype(F32)
    diag = iota((SUB, SUB), 0) == iota((SUB, SUB), 1)
    pos_row = (sub_pos_ref[...] & 7).astype(F32)
    pos_col = jnp.sum(jnp.where(diag, pos_row, 0.0), 1, keepdims=True) + 8.0 * iota(
        (SUB, 1), 0
    ).astype(F32)
    base_col = jnp.sum(jnp.where(diag, sub_base_ref[...].astype(F32), 0.0), 1, keepdims=True)
    at_sub = iota((SUB, TB), 1).astype(F32) == pos_col
    covered = jnp.sum(jnp.where(at_sub, 1.0, 0.0), 0, keepdims=True) > 0.5
    base = jnp.where(covered, jnp.sum(jnp.where(at_sub, base_col, 0.0), 0, keepdims=True), tok)
    sub_tok_col = jnp.sum(jnp.where(at_sub, tok, 0.0), 1, keepdims=True)
    eye = iota((TB, TB), 0) == iota((TB, TB), 1)

    def as_column(row):
        return jnp.sum(jnp.where(eye, row, 0.0), 1, keepdims=True)

    tok_col = as_column(tok)
    ids = jnp.concatenate([tok_col, sub_tok_col, base_col], 0)
    hot = (iota((TB + 2 * SUB, VOCAB), 1).astype(F32) == ids).astype(F32).astype(BF16)
    load_embed.wait()

    def squares(step, carry):
        plain, subs = carry
        part = embed_ref[:, pl.ds(pl.multiple_of(step * 256, 256), 256)]
        found = jnp.dot(hot, part, preferred_element_type=F32)
        plain_rows = found[:TB]
        plain_rows = plain_rows * plain_rows
        plain = plain + plain_rows[:, :TB] + plain_rows[:, TB:]
        e_tok = found[TB : TB + SUB]
        e_base = found[TB + SUB :]
        diff = e_tok - e_base
        new = []
        for a in range(NP):
            x = e_base + ALPHAS[a] * diff
            x = x * x
            new.append(subs[a] + x[:, :TB] + x[:, TB:])
        return plain, tuple(new)

    plain, subs = lax.fori_loop(
        0,
        D // 256,
        squares,
        (jnp.zeros((TB, TB), F32), tuple(jnp.zeros((SUB, TB), F32) for _ in range(NP))),
    )

    def inverse(total):
        return lax.rsqrt(jnp.sum(total, 1, keepdims=True) / D + 1e-06)

    plain_row = jnp.sum(jnp.where(eye, inverse(plain), 0.0), 0, keepdims=True)
    for a in range(NP):
        sub_row = jnp.sum(jnp.where(at_sub, inverse(subs[a]), 0.0), 0, keepdims=True)
        mine[a : a + 1, :] = jnp.where(covered, sub_row, plain_row)
    mine[4:5, :] = tok
    mine[5:6, :] = base
    mine[6:8, :] = jnp.zeros((2, TB), F32)
    info_ref[pl.ds(me, 1)] = mine[...].reshape(1, 8, TB)

    pl.semaphore_wait(barrier, 2 * NC + NP - 2 - own)

    @pl.loop(1, NC)
    def _(d):
        info_copy(d, lax.rem(me + d, NC), me).start()
        cols_copy(d, lax.rem(me + d, NC), me).start()

    lanes = pl.ds(pl.multiple_of(me * TB, TB), TB)

    def column(row):
        return jnp.broadcast_to(
            jnp.sum(jnp.where(chosen, row, 0.0), 1, keepdims=True), (CH, TB)
        )

    coef[0] = column(gain_ref[pl.ds(me, 1), :])
    coef[1] = column(skip_ref[...])
    for f in range(3):
        for j in range(3):
            taps[f * 3 + j] = column(taps_ref[f, j : j + 1, lanes].astype(F32))
    table[...] = nt_dot(pick, embed_ref[:, lanes])
    load_filter.wait()

    @pl.loop(0, NB // 8)
    def _(k):
        for n in range(2):
            at = pl.multiple_of(k * 8 * TB + n * 4 * TB, 4 * TB)
            rows = nt_dot(pick, filter_ref[pl.ds(at, 4 * TB), :].astype(BF16))
            for m in range(4):
                time_filter[8 * k + 4 * n + m] = rows[:, m * TB : (m + 1) * TB]

    vocab = iota((TB, VOCAB), 1).astype(F32)
    hot_tok = (vocab == tok_col).astype(F32).astype(BF16)
    hot_base = (vocab == as_column(base)).astype(F32).astype(BF16)

    @pl.loop(0, width // 256)
    def _(s):
        columns = pl.ds(pl.multiple_of(s * 256, 256), 256)
        part = embed_ref[:, pl.ds(pl.multiple_of(path * width + s * 256, 256), 256)]
        e_tok = jnp.dot(hot_tok, part, preferred_element_type=F32)
        e_base = jnp.dot(hot_base, part, preferred_element_type=F32)
        tok_out[:, columns] = e_tok.astype(BF16)
        base_out[:, columns] = e_base.astype(BF16)

    @pl.loop(1, NC)
    def _(d):
        dst = lax.rem(me + d, NC)
        src = lax.rem(me - d + NC, NC)
        info_copy(d, dst, src).wait_recv()
        cols_copy(d, dst, src).wait_recv()

    flip = (iota((TB, TB), 0) + iota((TB, TB), 1) == TB - 1).astype(F32).astype(BF16)
    past[...] = jnp.zeros_like(past)

    def forward(a, _):
        info = info_ref[a]
        e_tok = take_lanes(table[...], info[4:5].astype(jnp.int32))
        e_base = take_lanes(table[...], info[5:6].astype(jnp.int32))
        diff = e_tok - e_base
        e_base_s[a] = e_base
        diff_s[a] = diff
        cot = cols_ref[a].astype(F32)
        gain = coef[0]
        for p in range(NP):
            now = rounded((e_base + ALPHAS[p] * diff) * info[p : p + 1] * gain)
            one = pltpu.roll(now, 1, 1)
            two = pltpu.roll(now, 2, 1)
            now1 = jnp.where(lane < 1, past[p, 0], one)
            now2 = jnp.where(lane < 2, past[p, 1], two)
            past[p, 0] = one
            past[p, 1] = two
            q, k, v = (
                taps[f * 3] * now + taps[f * 3 + 1] * now1 + taps[f * 3 + 2] * now2
                for f in range(3)
            )
            key_s[a, p] = k
            val_s[a, p] = v
            stage[a, p * STRIDE : p * STRIDE + CH, :] = rounded(k * v)
            turn[a, p * CH : (p + 1) * CH, :] = (cot * q).astype(BF16)
        return 0

    def forward_pair(step, _):
        forward(2 * step, 0)
        forward(2 * step + 1, 0)
        return 0

    lax.fori_loop(0, NB // 2, forward_pair, 0)

    def flip_in(step, _):
        for n in range(FLIPS):
            a = step * FLIPS + n
            turned = jnp.dot(turn[a], flip, preferred_element_type=F32)
            for p in range(NP):
                at = (NP + p) * STRIDE
                stage[NB - 1 - a, at : at + CH, :] = turned[p * CH : (p + 1) * CH]
        return 0

    lax.fori_loop(0, NB // FLIPS, flip_in, 0)

    lane16 = iota((16, TB), 1)
    sub16 = iota((16, TB), 0)
    zero_tile = jnp.zeros((16, TB), BF16)

    def channel(c):
        rows = pl.ds(c, 8, stride=STRIDE)
        data = [
            jnp.concatenate([stage[2 * t, rows, :], stage[2 * t + 1, rows, :]], 0).astype(BF16)
            for t in range(NB // 2)
        ]
        before = jnp.zeros((16, TB), F32)
        rolled = [zero_tile] * 8
        blocks = []
        acc = None
        for k in range(NB):
            row = jnp.broadcast_to(time_filter[k, pl.ds(c, 1), :], (16, TB))
            turned = pltpu.roll(row, 0, 1, stride=1, stride_axis=0)
            shear = jnp.where(lane16 >= sub16, turned, before).astype(BF16)
            before = turned
            tiles = [shear]
            now = [shear]
            for g in range(1, TB // 16):
                moved = pltpu.roll(shear, 16 * g, 1)
                tiles.append(jnp.where(lane16 >= 16 * g, moved, rolled[g]))
                now.append(moved)
            rolled = now
            blocks.append(jnp.concatenate(tiles, 0))
            if k % (2 * CHUNK) == 2 * CHUNK - 1:
                first = k // 2 - CHUNK + 1
                rhs = jnp.concatenate(
                    [
                        jnp.concatenate([blocks[2 * n], blocks[2 * n + 1]], 1)
                        for n in range(CHUNK)
                    ],
                    0,
                )
                blocks = []
                lhs = jnp.concatenate(
                    [
                        jnp.concatenate([zero_tile] * n + data[: NB // 2 - n], 0)
                        for n in range(CHUNK)
                    ],
                    1,
                )
                size = 256 - 16 * first
                part = jnp.dot(lhs[:size], rhs, preferred_element_type=F32)
                if acc is None:
                    acc = part
                else:
                    acc = jnp.concatenate([acc[: 16 * first], acc[16 * first :] + part], 0)
                yield
        for a in range(NB):
            out = acc[8 * a : 8 * a + 8, :TB]
            if a > 0:
                out = out + acc[8 * a - 8 : 8 * a, TB:]
            conv[a, rows, :] = out

    def channels(step, _):
        running = [channel(step * UNROLL + n) for n in range(UNROLL)]
        while running:
            running = [x for x in running if next(x, "end") is None]
        return 0

    lax.fori_loop(0, CH // UNROLL, channels, 0)

    ahead[...] = jnp.zeros_like(ahead)

    def flip_out(step, _):
        for n in range(FLIPS):
            a = step * FLIPS + n
            got_rows = []
            for p in range(NP):
                rows = slice((NP + p) * STRIDE, (NP + p) * STRIDE + CH)
                got_rows.append((conv[a, rows, :] + coef[1] * stage[a, rows, :]).astype(BF16))
            grad_z[NB - 1 - a] = jnp.dot(
                jnp.concatenate(got_rows, 0), flip, preferred_element_type=F32
            )
        return 0

    lax.fori_loop(0, NB // FLIPS, flip_out, 0)

    def is_self(dst):
        return (to_path == path) & (dst == me)

    def backward(step, _):
        a = lax.rem(me + 1 - step + 2 * NB, NB)
        info = info_ref[a]
        cot = cols_ref[a].astype(F32)
        e_base = e_base_s[a]
        diff = diff_s[a]
        gain = coef[0]
        skip = coef[1]
        total = jnp.zeros((CH, TB), F32)
        sum_a = jnp.zeros((CH, TB), F32)
        sum_b = jnp.zeros((CH, TB), F32)
        for p in range(NP):
            rows = slice(p * STRIDE, p * STRIDE + CH)
            out = rounded(conv[a, rows, :] + skip * stage[a, rows, :])
            gz = grad_z[a, p * CH : (p + 1) * CH, :]
            gq = rounded(cot * out)
            gk = rounded(gz * val_s[a, p])
            gv = rounded(gz * key_s[a, p])
            u0, u1, u2 = (taps[j] * gq + taps[3 + j] * gk + taps[6 + j] * gv for j in range(3))
            one = pltpu.roll(u1, TB - 1, 1)
            two = pltpu.roll(u2, TB - 2, 1)
            gn = (
                u0
                + jnp.where(lane < TB - 1, one, ahead[p, 0])
                + jnp.where(lane < TB - 2, two, ahead[p, 1])
            )
            ahead[p, 0] = one
            ahead[p, 1] = two
            inv = info[p : p + 1]
            scaled = gain * gn
            total = total + inv * scaled
            w = (e_base + ALPHAS[p] * diff) * scaled * (inv * inv * inv)
            sum_a = sum_a + w
            sum_b = sum_b + ALPHAS[p] * w

        @pl.when(step > 0)
        def _():
            sums[a] = total.astype(BF16)
            ab[a, 0:1, :] = jnp.sum(sum_a, 0, keepdims=True)
            ab[a, 1:2, :] = jnp.sum(sum_b, 0, keepdims=True)

            @pl.when(jnp.logical_not(is_self(a)))
            def _():
                ab_copy(a, slot, slot).start()
                sums_copy(a, slot, slot).start()

            @pl.when(is_self(a))
            def _():
                got[pl.ds(slot, 1)] = sums[pl.ds(a, 1)]
                got_ab[pl.ds(slot, 1)] = ab[pl.ds(a, 1)]

        @pl.when(a == 0)
        def _():
            ahead[...] = jnp.zeros_like(ahead)

        return 0

    lax.fori_loop(0, NB + 1, backward, 0)

    def others(s):
        return jnp.logical_not((to_path == path) & (s == slot))

    @pl.loop(0, NC)
    def _(s):
        @pl.when(others(s))
        def _():
            ab_copy(me, s, s).wait_recv()

    own_ab[...] = jnp.sum(got_ab[...], 0)

    @pl.loop(1, NP)
    def _(d):
        group_copy(d, path).start()

    @pl.loop(0, NC)
    def _(s):
        @pl.when(others(s))
        def _():
            sums_copy(me, s, s).wait_recv()

    both = own_ab[...]
    for d in range(1, NP):
        src = lax.rem(path - d + NP, NP)
        group_copy(d, src).wait_recv()
        both = both + group_ab[pl.ds(src, 1)][0]
    both_out[...] = both
    sums_out[...] = got[...]

    @pl.loop(1, NC)
    def _(d):
        dst = lax.rem(me + d, NC)
        info_copy(d, dst, me).wait_send()
        cols_copy(d, dst, me).wait_send()

    @pl.loop(0, NC)
    def _(d):
        @pl.when(jnp.logical_not(is_self(d)))
        def _():
            ab_copy(d, slot, slot).wait_send()
            sums_copy(d, slot, slot).wait_send()

    @pl.loop(1, NP)
    def _(d):
        group_copy(d, path).wait_send()


def output_kernel(sums_ref, both_ref, tok_ref, base_ref, grad_ref, attr_ref):
    eye = iota((TB, TB), 0) == iota((TB, TB), 1)
    unit = eye.astype(F32).astype(BF16)
    scale = 1.0 / (NP * D)

    def as_column(row):
        return jnp.sum(jnp.where(eye, row, 0.0), 1, keepdims=True) * scale

    a_col = as_column(both_ref[0:1])
    b_col = as_column(both_ref[1:2])
    for n in range(OUT // TB):
        columns = slice(n * TB, (n + 1) * TB)
        summed = nt_dot(unit, sums_ref[4 * n : 4 * n + 4].reshape(TB, TB))
        e_base = base_ref[:, columns].astype(F32)
        diff = tok_ref[:, columns].astype(F32) - e_base
        grad = summed * (1.0 / NP) - (e_base * a_col + diff * b_col)
        grad_ref[:, columns] = grad
        attr_ref[:, columns] = diff * grad


def body(tokens, sub_pos, sub_base, embed, norm_gain, fir_taps, long_filter, skip_gain, cotangent):
    vmem = pl.BlockSpec(memory_space=pltpu.VMEM)
    here = pl.BlockSpec(memory_space=pl.ANY)
    width = D // NP
    rows = jax.ShapeDtypeStruct((TB, width), BF16)
    dma = pltpu.SemaphoreType.DMA
    sums, both, e_tok, e_base = pl.pallas_call(
        fused_kernel,
        name="fused_stage",
        out_shape=(
            jax.ShapeDtypeStruct((NC, CH, TB), BF16),
            jax.ShapeDtypeStruct((2, TB), F32),
            rows,
            rows,
        ),
        in_specs=[vmem, vmem, vmem, here, vmem, vmem, here, vmem, here],
        out_specs=(vmem, vmem, vmem, vmem),
        scratch_shapes=[
            pltpu.VMEM((VOCAB, D), BF16),
            pltpu.VMEM((NB * TB, TB), F32),
            pltpu.VMEM((TB, D), BF16),
            pltpu.VMEM((8, TB), F32),
            pltpu.VMEM((NC, CH, TB), BF16),
            pltpu.VMEM((NC, 8, TB), F32),
            pltpu.VMEM((NC, CH, TB), BF16),
            pltpu.VMEM((CH, VOCAB), F32),
            pltpu.VMEM((9, CH, TB), F32),
            pltpu.VMEM((2, CH, TB), F32),
            pltpu.VMEM((NB, CH, TB), F32),
            pltpu.VMEM((NB, CH, TB), F32),
            pltpu.VMEM((NB, CH, TB), F32),
            pltpu.VMEM((NB, NP, CH, TB), F32),
            pltpu.VMEM((NB, NP, CH, TB), F32),
            pltpu.VMEM((NB, 2 * NP * STRIDE, TB), F32),
            pltpu.VMEM((NB, 2 * NP * STRIDE, TB), F32),
            pltpu.VMEM((NP, 2, CH, TB), F32),
            pltpu.VMEM((NP, 2, CH, TB), F32),
            pltpu.VMEM((NC, CH, TB), BF16),
            pltpu.VMEM((NC, 2, TB), F32),
            pltpu.VMEM((NC, CH, TB), BF16),
            pltpu.VMEM((NC, 2, TB), F32),
            pltpu.VMEM((2, TB), F32),
            pltpu.VMEM((NP, 2, TB), F32),
            pltpu.VMEM((NB, NP * CH, TB), BF16),
            pltpu.VMEM((NB, NP * CH, TB), F32),
            dma((3,)),
            dma((NC,)),
            dma((NC,)),
            dma((NC,)),
            dma((NC,)),
            dma((NC,)),
            dma((NC,)),
            dma((NC,)),
            dma((NC,)),
            dma((NP,)),
            dma((NP,)),
        ],
        compiler_params=pltpu.CompilerParams(
            collective_id=0, has_side_effects=True, vmem_limit_bytes=VMEM_LIMIT
        ),
    )(
        tokens.reshape(1, -1),
        sub_pos.reshape(1, -1),
        sub_base.reshape(1, -1),
        embed,
        norm_gain.reshape(-1, TB),
        fir_taps,
        long_filter,
        skip_gain.reshape(1, -1),
        cotangent,
    )
    block = pl.BlockSpec((TB, OUT), lambda i: (0, i))
    shape = jax.ShapeDtypeStruct((TB, width), F32)
    return pl.pallas_call(
        output_kernel,
        name="output_stage",
        grid=(width // OUT,),
        out_shape=(shape, shape),
        in_specs=[
            pl.BlockSpec((OUT // CH, CH, TB), lambda i: (i, 0, 0)),
            pl.BlockSpec((2, TB), lambda i: (0, 0)),
            block,
            block,
        ],
        out_specs=(block, block),
    )(sums, both, e_tok, e_base)


def solution(mesh):
    return jax.shard_map(
        body,
        mesh=mesh,
        in_specs=(
            P("ctx"),
            P("ctx"),
            P("ctx"),
            P(),
            P(),
            P(),
            P(None, "ctx"),
            P("ctx"),
            P("ctx", None),
        ),
        out_specs=(P("ctx", "path"), P("ctx", "path")),
        check_vma=False,
    )
```

```python
import jax
import jax.numpy as jnp
from jax import lax
from jax.experimental import pallas as pl
from jax.experimental.pallas import tpu as pltpu
from jax.sharding import PartitionSpec as P

MESH = pl.DeviceIdType.MESH
F32 = jnp.float32
BF16 = jnp.bfloat16

NP = 4
NC = 32
TB = 128
CH = 32
NB = 32
SUB = 16
VOCAB = 512
D = 4096
REACH = 2
STRIDE = CH + 1
UNROLL = 1
CHUNK = 2
FLIPS = 4
OUT = 512
ALPHAS = tuple((a + 0.5) / NP for a in range(NP))
VMEM_LIMIT = 60 * 1024 * 1024


def iota(shape, dim):
    return lax.broadcasted_iota(jnp.int32, shape, dim)


def rounded(x):
    return x.astype(BF16).astype(F32)


def nt_dot(a, b):
    return lax.dot_general(a, b, (((1,), (1,)), ((), ())), preferred_element_type=F32)


def take_lanes(table, index):
    rows = table.shape[0]
    low = jnp.broadcast_to(index & (TB - 1), (8, TB))
    high = jnp.broadcast_to(index >> 7, (8, TB))
    out = []
    for r in range(0, rows, 8):
        got = jnp.take_along_axis(table[r : r + 8, :TB], low, axis=1)
        for v in range(1, VOCAB // TB):
            more = jnp.take_along_axis(table[r : r + 8, v * TB : (v + 1) * TB], low, axis=1)
            got = jnp.where(high == v, more, got)
        out.append(got)
    return jnp.concatenate(out, 0)


def fused_kernel(
    tok_ref,
    sub_pos_ref,
    sub_base_ref,
    embed_hbm,
    gain_ref,
    taps_ref,
    filter_hbm,
    skip_ref,
    cot_hbm,
    sums_out,
    both_out,
    tok_out,
    base_out,
    embed_ref,
    filter_ref,
    cot_ref,
    mine,
    parts,
    info_ref,
    cols_ref,
    table,
    taps,
    coef,
    time_filter,
    e_base_s,
    diff_s,
    key_s,
    val_s,
    stage,
    conv,
    past,
    ahead,
    sums,
    ab,
    got,
    got_ab,
    own_ab,
    group_ab,
    turn,
    grad_z,
    shears,
    load_sem,
    info_send,
    info_recv,
    cols_send,
    cols_recv,
    sums_send,
    sums_recv,
    ab_send,
    ab_recv,
    group_send,
    group_recv,
):
    path = lax.axis_index("path")
    me = lax.axis_index("ctx")
    width = D // NP
    to_path = me // 8
    slot = (me % 8) * NP + path
    own = jnp.where(to_path == path, 1, 0)

    def partner(ctx):
        return jnp.where(ctx // 4 % 2 == me // 4 % 2, path, lax.rem(path + 2, NP))

    load_cot = pltpu.make_async_copy(cot_hbm, cot_ref, load_sem.at[0])
    load_embed = pltpu.make_async_copy(embed_hbm, embed_ref, load_sem.at[1])
    load_filter = pltpu.make_async_copy(filter_hbm, filter_ref, load_sem.at[2])
    load_cot.start()
    load_embed.start()
    load_filter.start()

    barrier = pltpu.get_barrier_semaphore()

    @pl.loop(1, NC)
    def _(d):
        other = lax.rem(me + d, NC)
        pl.semaphore_signal(
            barrier,
            inc=1,
            device_id={"path": partner(other), "ctx": other},
            device_id_type=MESH,
        )

    @pl.loop(0, NC)
    def _(s):
        src_path = lax.rem(s, NP)
        src_ctx = path * 8 + s // NP

        @pl.when((src_path != path) | (src_ctx != me))
        def _():
            pl.semaphore_signal(
                barrier,
                inc=1,
                device_id={"path": src_path, "ctx": src_ctx},
                device_id_type=MESH,
            )

    @pl.loop(1, NP)
    def _(d):
        pl.semaphore_signal(
            barrier, inc=1, device_id={"path": lax.rem(path + d, NP)}, device_id_type=MESH
        )

    def cols_copy(d, dst, at):
        return pltpu.make_async_remote_copy(
            src_ref=parts.at[dst],
            dst_ref=cols_ref.at[at],
            send_sem=cols_send.at[d],
            recv_sem=cols_recv.at[d],
            device_id={"path": partner(dst), "ctx": dst},
            device_id_type=MESH,
        )

    def info_copy(d, dst, at):
        return pltpu.make_async_remote_copy(
            src_ref=mine,
            dst_ref=info_ref.at[at],
            send_sem=info_send.at[d],
            recv_sem=info_recv.at[d],
            device_id={"path": partner(dst), "ctx": dst},
            device_id_type=MESH,
        )

    def sums_copy(dst, at, number):
        return pltpu.make_async_remote_copy(
            src_ref=sums.at[dst],
            dst_ref=got.at[at],
            send_sem=sums_send.at[dst],
            recv_sem=sums_recv.at[number],
            device_id={"path": to_path, "ctx": dst},
            device_id_type=MESH,
        )

    def ab_copy(dst, at, number):
        return pltpu.make_async_remote_copy(
            src_ref=ab.at[dst],
            dst_ref=got_ab.at[at],
            send_sem=ab_send.at[dst],
            recv_sem=ab_recv.at[number],
            device_id={"path": to_path, "ctx": dst},
            device_id_type=MESH,
        )

    def group_copy(d, at):
        return pltpu.make_async_remote_copy(
            src_ref=own_ab,
            dst_ref=group_ab.at[at],
            send_sem=group_send.at[d],
            recv_sem=group_recv.at[d],
            device_id={"path": lax.rem(path + d, NP)},
            device_id_type=MESH,
        )

    lane = iota((CH, TB), 1)
    chosen = lane == iota((CH, TB), 0) + path * CH
    pick = chosen.astype(F32).astype(BF16)
    load_cot.wait()

    @pl.loop(0, NC // 4)
    def _(step):
        to = partner(4 * step)
        want = (lane == iota((CH, TB), 0) + to * CH).astype(F32).astype(BF16)
        for n in range(4):
            block = cot_ref[:, pl.ds(pl.multiple_of((4 * step + n) * TB, TB), TB)]
            parts[4 * step + n] = nt_dot(want, block).astype(BF16)

    cols_ref[pl.ds(me, 1)] = parts[pl.ds(me, 1)]

    tok = tok_ref[...].astype(F32)
    diag = iota((SUB, SUB), 0) == iota((SUB, SUB), 1)
    pos_row = (sub_pos_ref[...] & 7).astype(F32)
    pos_col = jnp.sum(jnp.where(diag, pos_row, 0.0), 1, keepdims=True) + 8.0 * iota(
        (SUB, 1), 0
    ).astype(F32)
    base_col = jnp.sum(jnp.where(diag, sub_base_ref[...].astype(F32), 0.0), 1, keepdims=True)
    at_sub = iota((SUB, TB), 1).astype(F32) == pos_col
    covered = jnp.sum(jnp.where(at_sub, 1.0, 0.0), 0, keepdims=True) > 0.5
    base = jnp.where(covered, jnp.sum(jnp.where(at_sub, base_col, 0.0), 0, keepdims=True), tok)
    sub_tok_col = jnp.sum(jnp.where(at_sub, tok, 0.0), 1, keepdims=True)
    eye = iota((TB, TB), 0) == iota((TB, TB), 1)

    def as_column(row):
        return jnp.sum(jnp.where(eye, row, 0.0), 1, keepdims=True)

    tok_col = as_column(tok)
    ids = jnp.concatenate([tok_col, sub_tok_col, base_col], 0)
    hot = (iota((TB + 2 * SUB, VOCAB), 1).astype(F32) == ids).astype(F32).astype(BF16)
    load_embed.wait()

    def squares(step, carry):
        plain, subs = carry
        part = embed_ref[:, pl.ds(pl.multiple_of(step * 256, 256), 256)]
        found = jnp.dot(hot, part, preferred_element_type=F32)
        plain_rows = found[:TB]
        plain_rows = plain_rows * plain_rows
        plain = plain + plain_rows[:, :TB] + plain_rows[:, TB:]
        e_tok = found[TB : TB + SUB]
        e_base = found[TB + SUB :]
        diff = e_tok - e_base
        new = []
        for a in range(NP):
            x = e_base + ALPHAS[a] * diff
            x = x * x
            new.append(subs[a] + x[:, :TB] + x[:, TB:])
        return plain, tuple(new)

    plain, subs = lax.fori_loop(
        0,
        D // 256,
        squares,
        (jnp.zeros((TB, TB), F32), tuple(jnp.zeros((SUB, TB), F32) for _ in range(NP))),
    )

    def inverse(total):
        return lax.rsqrt(jnp.sum(total, 1, keepdims=True) / D + 1e-06)

    plain_row = jnp.sum(jnp.where(eye, inverse(plain), 0.0), 0, keepdims=True)
    for a in range(NP):
        sub_row = jnp.sum(jnp.where(at_sub, inverse(subs[a]), 0.0), 0, keepdims=True)
        mine[a : a + 1, :] = jnp.where(covered, sub_row, plain_row)
    mine[4:5, :] = tok
    mine[5:6, :] = base
    mine[6:8, :] = jnp.zeros((2, TB), F32)
    info_ref[pl.ds(me, 1)] = mine[...].reshape(1, 8, TB)

    pl.semaphore_wait(barrier, 2 * NC + NP - 2 - own)

    @pl.loop(1, NC)
    def _(d):
        info_copy(d, lax.rem(me + d, NC), me).start()
        cols_copy(d, lax.rem(me + d, NC), me).start()

    lanes = pl.ds(pl.multiple_of(me * TB, TB), TB)

    def column(row):
        return jnp.broadcast_to(
            jnp.sum(jnp.where(chosen, row, 0.0), 1, keepdims=True), (CH, TB)
        )

    coef[0] = column(gain_ref[pl.ds(me, 1), :])
    coef[1] = column(skip_ref[...])
    for f in range(3):
        for j in range(3):
            taps[f * 3 + j] = column(taps_ref[f, j : j + 1, lanes].astype(F32))
    table[...] = nt_dot(pick, embed_ref[:, lanes])
    load_filter.wait()

    @pl.loop(0, NB // 8)
    def _(k):
        for n in range(2):
            at = pl.multiple_of(k * 8 * TB + n * 4 * TB, 4 * TB)
            rows = nt_dot(pick, filter_ref[pl.ds(at, 4 * TB), :].astype(BF16))
            for m in range(4):
                time_filter[8 * k + 4 * n + m] = rows[:, m * TB : (m + 1) * TB]

    vocab = iota((TB, VOCAB), 1).astype(F32)
    hot_tok = (vocab == tok_col).astype(F32).astype(BF16)
    hot_base = (vocab == as_column(base)).astype(F32).astype(BF16)

    @pl.loop(0, width // 256)
    def _(s):
        columns = pl.ds(pl.multiple_of(s * 256, 256), 256)
        part = embed_ref[:, pl.ds(pl.multiple_of(path * width + s * 256, 256), 256)]
        e_tok = jnp.dot(hot_tok, part, preferred_element_type=F32)
        e_base = jnp.dot(hot_base, part, preferred_element_type=F32)
        tok_out[:, columns] = e_tok.astype(BF16)
        base_out[:, columns] = e_base.astype(BF16)

    lane16 = iota((16, TB), 1)
    sub16 = iota((16, TB), 0)

    def shear_channel(c, _):
        before = jnp.zeros((16, TB), F32)
        for k in range(NB):
            row = jnp.broadcast_to(time_filter[k, pl.ds(c, 1), :], (16, TB))
            turned = pltpu.roll(row, 0, 1, stride=1, stride_axis=0)
            shears[c, 16 * k : 16 * k + 16, :] = jnp.where(
                lane16 >= sub16, turned, before
            ).astype(BF16)
            before = turned
        return 0

    lax.fori_loop(0, CH, shear_channel, 0)

    @pl.loop(1, NC)
    def _(d):
        dst = lax.rem(me + d, NC)
        src = lax.rem(me - d + NC, NC)
        info_copy(d, dst, src).wait_recv()
        cols_copy(d, dst, src).wait_recv()

    flip = (iota((TB, TB), 0) + iota((TB, TB), 1) == TB - 1).astype(F32).astype(BF16)
    past[...] = jnp.zeros_like(past)

    def forward(a, _):
        info = info_ref[a]
        e_tok = take_lanes(table[...], info[4:5].astype(jnp.int32))
        e_base = take_lanes(table[...], info[5:6].astype(jnp.int32))
        diff = e_tok - e_base
        e_base_s[a] = e_base
        diff_s[a] = diff
        cot = cols_ref[a].astype(F32)
        gain = coef[0]
        for p in range(NP):
            now = rounded((e_base + ALPHAS[p] * diff) * info[p : p + 1] * gain)
            one = pltpu.roll(now, 1, 1)
            two = pltpu.roll(now, 2, 1)
            now1 = jnp.where(lane < 1, past[p, 0], one)
            now2 = jnp.where(lane < 2, past[p, 1], two)
            past[p, 0] = one
            past[p, 1] = two
            q, k, v = (
                taps[f * 3] * now + taps[f * 3 + 1] * now1 + taps[f * 3 + 2] * now2
                for f in range(3)
            )
            key_s[a, p] = k
            val_s[a, p] = v
            stage[a, p * STRIDE : p * STRIDE + CH, :] = rounded(k * v)
            turn[a, p * CH : (p + 1) * CH, :] = (cot * q).astype(BF16)
        return 0

    def forward_pair(step, _):
        forward(2 * step, 0)
        forward(2 * step + 1, 0)
        return 0

    lax.fori_loop(0, NB // 2, forward_pair, 0)

    def flip_in(step, _):
        for n in range(FLIPS):
            a = step * FLIPS + n
            turned = jnp.dot(turn[a], flip, preferred_element_type=F32)
            for p in range(NP):
                at = (NP + p) * STRIDE
                stage[NB - 1 - a, at : at + CH, :] = turned[p * CH : (p + 1) * CH]
        return 0

    lax.fori_loop(0, NB // FLIPS, flip_in, 0)

    low16 = lane16 < TB // 2
    low8 = iota((8, TB), 1) < TB // 2
    zero_tile = jnp.zeros((16, TB), BF16)

    def channel(c):
        rows = pl.ds(c, 8, stride=STRIDE)
        even, odd = [], []
        data = turned_data = zero_tile
        for t in range(NB // 2):
            tile = jnp.concatenate(
                [stage[2 * t, rows, :], stage[2 * t + 1, rows, :]], 0
            ).astype(BF16)
            swapped = pltpu.roll(tile, TB // 2, 1)
            even.append(jnp.where(low16, tile, turned_data))
            odd.append(jnp.where(low16, swapped, data))
            data, turned_data = tile, swapped
        rolled = [zero_tile] * 4
        blocks = []
        acc = None
        for k in range(NB):
            shear = shears[c, 16 * k : 16 * k + 16, :]
            tiles = [shear]
            now = [shear]
            for g in range(1, 4):
                moved = pltpu.roll(shear, 16 * g, 1)
                tiles.append(jnp.where(lane16 >= 16 * g, moved, rolled[g]))
                now.append(moved)
            rolled = now
            blocks.append(jnp.concatenate(tiles, 0))
            if k % (4 * CHUNK) == 4 * CHUNK - 1:
                first = k // 4 - CHUNK + 1
                rhs = jnp.concatenate(
                    [
                        jnp.concatenate([blocks[2 * n], blocks[2 * n + 1]], 1)
                        for n in range(2 * CHUNK)
                    ],
                    0,
                )
                blocks = []
                count = NB // 2 - 2 * first
                lhs = jnp.concatenate(
                    [
                        jnp.concatenate(
                            ([zero_tile] * (2 * n) + even)[:count]
                            + ([zero_tile] * (2 * n) + odd)[:count],
                            0,
                        )
                        for n in range(CHUNK)
                    ],
                    1,
                )
                part = jnp.dot(lhs, rhs, preferred_element_type=F32)
                if acc is None:
                    acc = part
                else:
                    skip_rows = 32 * first
                    acc = jnp.concatenate(
                        [
                            acc[:skip_rows],
                            acc[skip_rows:256] + part[: 16 * count],
                            acc[256 : 256 + skip_rows],
                            acc[256 + skip_rows :] + part[16 * count :],
                        ],
                        0,
                    )
        last = jnp.zeros((8, TB), F32)
        for a in range(NB):
            out = acc[8 * a : 8 * a + 8, :TB]
            side = acc[256 + 8 * a : 264 + 8 * a, :TB]
            if a > 0:
                out = out + acc[8 * a - 8 : 8 * a, TB:]
                side = side + acc[248 + 8 * a : 256 + 8 * a, TB:]
            swapped = pltpu.roll(side, TB // 2, 1)
            conv[a, rows, :] = out + jnp.where(low8, last, swapped)
            last = swapped

    def channels(step, _):
        for n in range(UNROLL):
            channel(step * UNROLL + n)
        return 0

    lax.fori_loop(0, CH // UNROLL, channels, 0)

    ahead[...] = jnp.zeros_like(ahead)

    def flip_out(step, _):
        for n in range(FLIPS):
            a = step * FLIPS + n
            got_rows = []
            for p in range(NP):
                rows = slice((NP + p) * STRIDE, (NP + p) * STRIDE + CH)
                got_rows.append((conv[a, rows, :] + coef[1] * stage[a, rows, :]).astype(BF16))
            grad_z[NB - 1 - a] = jnp.dot(
                jnp.concatenate(got_rows, 0), flip, preferred_element_type=F32
            )
        return 0

    lax.fori_loop(0, NB // FLIPS, flip_out, 0)

    def is_self(dst):
        return (to_path == path) & (dst == me)

    def backward(step, _):
        a = lax.rem(me + 1 - step + 2 * NB, NB)
        info = info_ref[a]
        cot = cols_ref[a].astype(F32)
        e_base = e_base_s[a]
        diff = diff_s[a]
        gain = coef[0]
        skip = coef[1]
        total = jnp.zeros((CH, TB), F32)
        sum_a = jnp.zeros((CH, TB), F32)
        sum_b = jnp.zeros((CH, TB), F32)
        for p in range(NP):
            rows = slice(p * STRIDE, p * STRIDE + CH)
            out = rounded(conv[a, rows, :] + skip * stage[a, rows, :])
            gz = grad_z[a, p * CH : (p + 1) * CH, :]
            gq = rounded(cot * out)
            gk = rounded(gz * val_s[a, p])
            gv = rounded(gz * key_s[a, p])
            u0, u1, u2 = (taps[j] * gq + taps[3 + j] * gk + taps[6 + j] * gv for j in range(3))
            one = pltpu.roll(u1, TB - 1, 1)
            two = pltpu.roll(u2, TB - 2, 1)
            gn = (
                u0
                + jnp.where(lane < TB - 1, one, ahead[p, 0])
                + jnp.where(lane < TB - 2, two, ahead[p, 1])
            )
            ahead[p, 0] = one
            ahead[p, 1] = two
            inv = info[p : p + 1]
            scaled = gain * gn
            total = total + inv * scaled
            w = (e_base + ALPHAS[p] * diff) * scaled * (inv * inv * inv)
            sum_a = sum_a + w
            sum_b = sum_b + ALPHAS[p] * w

        @pl.when(step > 0)
        def _():
            sums[a] = total.astype(BF16)
            ab[a, 0:1, :] = jnp.sum(sum_a, 0, keepdims=True)
            ab[a, 1:2, :] = jnp.sum(sum_b, 0, keepdims=True)

            @pl.when(jnp.logical_not(is_self(a)))
            def _():
                ab_copy(a, slot, slot).start()
                sums_copy(a, slot, slot).start()

            @pl.when(is_self(a))
            def _():
                got[pl.ds(slot, 1)] = sums[pl.ds(a, 1)]
                got_ab[pl.ds(slot, 1)] = ab[pl.ds(a, 1)]

        @pl.when(a == 0)
        def _():
            ahead[...] = jnp.zeros_like(ahead)

        return 0

    lax.fori_loop(0, NB + 1, backward, 0)

    def others(s):
        return jnp.logical_not((to_path == path) & (s == slot))

    @pl.loop(0, NC)
    def _(s):
        @pl.when(others(s))
        def _():
            ab_copy(me, s, s).wait_recv()

    own_ab[...] = jnp.sum(got_ab[...], 0)

    @pl.loop(1, NP)
    def _(d):
        group_copy(d, path).start()

    @pl.loop(0, NC)
    def _(s):
        @pl.when(others(s))
        def _():
            sums_copy(me, s, s).wait_recv()

    both = own_ab[...]
    for d in range(1, NP):
        src = lax.rem(path - d + NP, NP)
        group_copy(d, src).wait_recv()
        both = both + group_ab[pl.ds(src, 1)][0]
    both_out[...] = both
    sums_out[...] = got[...]

    @pl.loop(1, NC)
    def _(d):
        dst = lax.rem(me + d, NC)
        info_copy(d, dst, me).wait_send()
        cols_copy(d, dst, me).wait_send()

    @pl.loop(0, NC)
    def _(d):
        @pl.when(jnp.logical_not(is_self(d)))
        def _():
            ab_copy(d, slot, slot).wait_send()
            sums_copy(d, slot, slot).wait_send()

    @pl.loop(1, NP)
    def _(d):
        group_copy(d, path).wait_send()


def output_kernel(sums_ref, both_ref, tok_ref, base_ref, grad_ref, attr_ref):
    eye = iota((TB, TB), 0) == iota((TB, TB), 1)
    unit = eye.astype(F32).astype(BF16)
    scale = 1.0 / (NP * D)

    def as_column(row):
        return jnp.sum(jnp.where(eye, row, 0.0), 1, keepdims=True) * scale

    a_col = as_column(both_ref[0:1])
    b_col = as_column(both_ref[1:2])
    for n in range(OUT // TB):
        columns = slice(n * TB, (n + 1) * TB)
        summed = nt_dot(unit, sums_ref[4 * n : 4 * n + 4].reshape(TB, TB))
        e_base = base_ref[:, columns].astype(F32)
        diff = tok_ref[:, columns].astype(F32) - e_base
        grad = summed * (1.0 / NP) - (e_base * a_col + diff * b_col)
        grad_ref[:, columns] = grad
        attr_ref[:, columns] = diff * grad


def body(tokens, sub_pos, sub_base, embed, norm_gain, fir_taps, long_filter, skip_gain, cotangent):
    vmem = pl.BlockSpec(memory_space=pltpu.VMEM)
    here = pl.BlockSpec(memory_space=pl.ANY)
    width = D // NP
    rows = jax.ShapeDtypeStruct((TB, width), BF16)
    dma = pltpu.SemaphoreType.DMA
    sums, both, e_tok, e_base = pl.pallas_call(
        fused_kernel,
        name="fused_stage",
        out_shape=(
            jax.ShapeDtypeStruct((NC, CH, TB), BF16),
            jax.ShapeDtypeStruct((2, TB), F32),
            rows,
            rows,
        ),
        in_specs=[vmem, vmem, vmem, here, vmem, vmem, here, vmem, here],
        out_specs=(vmem, vmem, vmem, vmem),
        scratch_shapes=[
            pltpu.VMEM((VOCAB, D), BF16),
            pltpu.VMEM((NB * TB, TB), F32),
            pltpu.VMEM((TB, D), BF16),
            pltpu.VMEM((8, TB), F32),
            pltpu.VMEM((NC, CH, TB), BF16),
            pltpu.VMEM((NC, 8, TB), F32),
            pltpu.VMEM((NC, CH, TB), BF16),
            pltpu.VMEM((CH, VOCAB), F32),
            pltpu.VMEM((9, CH, TB), F32),
            pltpu.VMEM((2, CH, TB), F32),
            pltpu.VMEM((NB, CH, TB), F32),
            pltpu.VMEM((NB, CH, TB), F32),
            pltpu.VMEM((NB, CH, TB), F32),
            pltpu.VMEM((NB, NP, CH, TB), F32),
            pltpu.VMEM((NB, NP, CH, TB), F32),
            pltpu.VMEM((NB, 2 * NP * STRIDE, TB), F32),
            pltpu.VMEM((NB, 2 * NP * STRIDE, TB), F32),
            pltpu.VMEM((NP, 2, CH, TB), F32),
            pltpu.VMEM((NP, 2, CH, TB), F32),
            pltpu.VMEM((NC, CH, TB), BF16),
            pltpu.VMEM((NC, 2, TB), F32),
            pltpu.VMEM((NC, CH, TB), BF16),
            pltpu.VMEM((NC, 2, TB), F32),
            pltpu.VMEM((2, TB), F32),
            pltpu.VMEM((NP, 2, TB), F32),
            pltpu.VMEM((NB, NP * CH, TB), BF16),
            pltpu.VMEM((NB, NP * CH, TB), F32),
            pltpu.VMEM((CH, NB * 16, TB), BF16),
            dma((3,)),
            dma((NC,)),
            dma((NC,)),
            dma((NC,)),
            dma((NC,)),
            dma((NC,)),
            dma((NC,)),
            dma((NC,)),
            dma((NC,)),
            dma((NP,)),
            dma((NP,)),
        ],
        compiler_params=pltpu.CompilerParams(
            collective_id=0, has_side_effects=True, vmem_limit_bytes=VMEM_LIMIT
        ),
    )(
        tokens.reshape(1, -1),
        sub_pos.reshape(1, -1),
        sub_base.reshape(1, -1),
        embed,
        norm_gain.reshape(-1, TB),
        fir_taps,
        long_filter,
        skip_gain.reshape(1, -1),
        cotangent,
    )
    block = pl.BlockSpec((TB, OUT), lambda i: (0, i))
    shape = jax.ShapeDtypeStruct((TB, width), F32)
    return pl.pallas_call(
        output_kernel,
        name="output_stage",
        grid=(width // OUT,),
        out_shape=(shape, shape),
        in_specs=[
            pl.BlockSpec((OUT // CH, CH, TB), lambda i: (i, 0, 0)),
            pl.BlockSpec((2, TB), lambda i: (0, 0)),
            block,
            block,
        ],
        out_specs=(block, block),
    )(sums, both, e_tok, e_base)


def solution(mesh):
    return jax.shard_map(
        body,
        mesh=mesh,
        in_specs=(
            P("ctx"),
            P("ctx"),
            P("ctx"),
            P(),
            P(),
            P(),
            P(None, "ctx"),
            P("ctx"),
            P("ctx", None),
        ),
        out_specs=(P("ctx", "path"), P("ctx", "path")),
        check_vma=False,
    )
```

```python
import jax
import jax.numpy as jnp
from jax import lax
from jax.experimental import pallas as pl
from jax.experimental.pallas import tpu as pltpu
from jax.sharding import PartitionSpec as P

MESH = pl.DeviceIdType.MESH
F32 = jnp.float32
BF16 = jnp.bfloat16

NP = 4
NC = 32
TB = 128
CH = 32
NB = 32
SUB = 16
VOCAB = 512
D = 4096
REACH = 2
STRIDE = CH + 1
UNROLL = 8
CHUNK = 2
FLIPS = 8
OUT = 512
ALPHAS = tuple((a + 0.5) / NP for a in range(NP))
VMEM_LIMIT = 60 * 1024 * 1024


def iota(shape, dim):
    return lax.broadcasted_iota(jnp.int32, shape, dim)


def rounded(x):
    return x.astype(BF16).astype(F32)


def nt_dot(a, b):
    return lax.dot_general(a, b, (((1,), (1,)), ((), ())), preferred_element_type=F32)


def take_lanes(table, index):
    rows = table.shape[0]
    low = jnp.broadcast_to(index & (TB - 1), (8, TB))
    high = jnp.broadcast_to(index >> 7, (8, TB))
    out = []
    for r in range(0, rows, 8):
        got = jnp.take_along_axis(table[r : r + 8, :TB], low, axis=1)
        for v in range(1, VOCAB // TB):
            more = jnp.take_along_axis(table[r : r + 8, v * TB : (v + 1) * TB], low, axis=1)
            got = jnp.where(high == v, more, got)
        out.append(got)
    return jnp.concatenate(out, 0)


def fused_kernel(
    tok_ref,
    sub_pos_ref,
    sub_base_ref,
    embed_hbm,
    gain_ref,
    taps_ref,
    filter_hbm,
    skip_ref,
    cot_hbm,
    sums_out,
    both_out,
    tok_out,
    base_out,
    embed_ref,
    filter_ref,
    cot_ref,
    mine,
    parts,
    info_ref,
    cols_ref,
    table,
    taps,
    coef,
    time_filter,
    e_base_s,
    diff_s,
    key_s,
    val_s,
    stage,
    conv,
    past,
    ahead,
    sums,
    ab,
    got,
    got_ab,
    own_ab,
    group_ab,
    turn,
    grad_z,
    shears,
    load_sem,
    info_send,
    info_recv,
    cols_send,
    cols_recv,
    sums_send,
    sums_recv,
    ab_send,
    ab_recv,
    group_send,
    group_recv,
):
    path = lax.axis_index("path")
    me = lax.axis_index("ctx")
    width = D // NP
    to_path = me // 8
    slot = (me % 8) * NP + path
    own = jnp.where(to_path == path, 1, 0)

    def partner(ctx):
        return jnp.where(ctx // 4 % 2 == me // 4 % 2, path, lax.rem(path + 2, NP))

    load_cot = pltpu.make_async_copy(cot_hbm, cot_ref, load_sem.at[0])
    load_embed = pltpu.make_async_copy(embed_hbm, embed_ref, load_sem.at[1])
    load_filter = pltpu.make_async_copy(filter_hbm, filter_ref, load_sem.at[2])
    load_cot.start()
    load_embed.start()
    load_filter.start()

    barrier = pltpu.get_barrier_semaphore()

    @pl.loop(1, NC)
    def _(d):
        other = lax.rem(me + d, NC)
        pl.semaphore_signal(
            barrier,
            inc=1,
            device_id={"path": partner(other), "ctx": other},
            device_id_type=MESH,
        )

    @pl.loop(0, NC)
    def _(s):
        src_path = lax.rem(s, NP)
        src_ctx = path * 8 + s // NP

        @pl.when((src_path != path) | (src_ctx != me))
        def _():
            pl.semaphore_signal(
                barrier,
                inc=1,
                device_id={"path": src_path, "ctx": src_ctx},
                device_id_type=MESH,
            )

    @pl.loop(1, NP)
    def _(d):
        pl.semaphore_signal(
            barrier, inc=1, device_id={"path": lax.rem(path + d, NP)}, device_id_type=MESH
        )

    def cols_copy(d, dst, at):
        return pltpu.make_async_remote_copy(
            src_ref=parts.at[dst],
            dst_ref=cols_ref.at[at],
            send_sem=cols_send.at[d],
            recv_sem=cols_recv.at[d],
            device_id={"path": partner(dst), "ctx": dst},
            device_id_type=MESH,
        )

    def info_copy(d, dst, at):
        return pltpu.make_async_remote_copy(
            src_ref=mine,
            dst_ref=info_ref.at[at],
            send_sem=info_send.at[d],
            recv_sem=info_recv.at[d],
            device_id={"path": partner(dst), "ctx": dst},
            device_id_type=MESH,
        )

    def sums_copy(dst, at, number):
        return pltpu.make_async_remote_copy(
            src_ref=sums.at[dst],
            dst_ref=got.at[at],
            send_sem=sums_send.at[dst],
            recv_sem=sums_recv.at[number],
            device_id={"path": to_path, "ctx": dst},
            device_id_type=MESH,
        )

    def ab_copy(dst, at, number):
        return pltpu.make_async_remote_copy(
            src_ref=ab.at[dst],
            dst_ref=got_ab.at[at],
            send_sem=ab_send.at[dst],
            recv_sem=ab_recv.at[number],
            device_id={"path": to_path, "ctx": dst},
            device_id_type=MESH,
        )

    def group_copy(d, at):
        return pltpu.make_async_remote_copy(
            src_ref=own_ab,
            dst_ref=group_ab.at[at],
            send_sem=group_send.at[d],
            recv_sem=group_recv.at[d],
            device_id={"path": lax.rem(path + d, NP)},
            device_id_type=MESH,
        )

    lane = iota((CH, TB), 1)
    chosen = lane == iota((CH, TB), 0) + path * CH
    pick = chosen.astype(F32).astype(BF16)
    load_cot.wait()

    @pl.loop(0, NC // 4)
    def _(step):
        to = partner(4 * step)
        want = (lane == iota((CH, TB), 0) + to * CH).astype(F32).astype(BF16)
        for n in range(4):
            block = cot_ref[:, pl.ds(pl.multiple_of((4 * step + n) * TB, TB), TB)]
            parts[4 * step + n] = nt_dot(want, block).astype(BF16)

    cols_ref[pl.ds(me, 1)] = parts[pl.ds(me, 1)]

    tok = tok_ref[...].astype(F32)
    diag = iota((SUB, SUB), 0) == iota((SUB, SUB), 1)
    pos_row = (sub_pos_ref[...] & 7).astype(F32)
    pos_col = jnp.sum(jnp.where(diag, pos_row, 0.0), 1, keepdims=True) + 8.0 * iota(
        (SUB, 1), 0
    ).astype(F32)
    base_col = jnp.sum(jnp.where(diag, sub_base_ref[...].astype(F32), 0.0), 1, keepdims=True)
    at_sub = iota((SUB, TB), 1).astype(F32) == pos_col
    covered = jnp.sum(jnp.where(at_sub, 1.0, 0.0), 0, keepdims=True) > 0.5
    base = jnp.where(covered, jnp.sum(jnp.where(at_sub, base_col, 0.0), 0, keepdims=True), tok)
    sub_tok_col = jnp.sum(jnp.where(at_sub, tok, 0.0), 1, keepdims=True)
    eye = iota((TB, TB), 0) == iota((TB, TB), 1)

    def as_column(row):
        return jnp.sum(jnp.where(eye, row, 0.0), 1, keepdims=True)

    tok_col = as_column(tok)
    ids = jnp.concatenate([tok_col, sub_tok_col, base_col], 0)
    hot = (iota((TB + 2 * SUB, VOCAB), 1).astype(F32) == ids).astype(F32).astype(BF16)
    load_embed.wait()

    def squares(step, carry):
        plain, subs = carry
        for n in range(2):
            part = embed_ref[:, pl.ds(pl.multiple_of(step * 512 + n * 256, 256), 256)]
            found = jnp.dot(hot, part, preferred_element_type=F32)
            plain_rows = found[:TB]
            plain_rows = plain_rows * plain_rows
            plain = plain + (plain_rows[:, :TB] + plain_rows[:, TB:])
            e_tok = found[TB : TB + SUB]
            e_base = found[TB + SUB :]
            diff = e_tok - e_base
            new = []
            for a in range(NP):
                x = e_base + ALPHAS[a] * diff
                x = x * x
                new.append(subs[a] + (x[:, :TB] + x[:, TB:]))
            subs = tuple(new)
        return plain, subs

    plain, subs = lax.fori_loop(
        0,
        D // 512,
        squares,
        (jnp.zeros((TB, TB), F32), tuple(jnp.zeros((SUB, TB), F32) for _ in range(NP))),
    )

    def inverse(total):
        return lax.rsqrt(jnp.sum(total, 1, keepdims=True) / D + 1e-06)

    plain_row = jnp.sum(jnp.where(eye, inverse(plain), 0.0), 0, keepdims=True)
    for a in range(NP):
        sub_row = jnp.sum(jnp.where(at_sub, inverse(subs[a]), 0.0), 0, keepdims=True)
        mine[a : a + 1, :] = jnp.where(covered, sub_row, plain_row)
    mine[4:5, :] = tok
    mine[5:6, :] = base
    mine[6:8, :] = jnp.zeros((2, TB), F32)
    info_ref[pl.ds(me, 1)] = mine[...].reshape(1, 8, TB)

    pl.semaphore_wait(barrier, 2 * NC + NP - 2 - own)

    @pl.loop(1, NC)
    def _(d):
        info_copy(d, lax.rem(me + d, NC), me).start()
        cols_copy(d, lax.rem(me + d, NC), me).start()

    lanes = pl.ds(pl.multiple_of(me * TB, TB), TB)

    def column(row):
        return jnp.broadcast_to(
            jnp.sum(jnp.where(chosen, row, 0.0), 1, keepdims=True), (CH, TB)
        )

    coef[0] = column(gain_ref[pl.ds(me, 1), :])
    coef[1] = column(skip_ref[...])
    for f in range(3):
        for j in range(3):
            taps[f * 3 + j] = column(taps_ref[f, j : j + 1, lanes].astype(F32))
    table[...] = nt_dot(pick, embed_ref[:, lanes])
    load_filter.wait()

    @pl.loop(0, NB // 8)
    def _(k):
        for n in range(2):
            at = pl.multiple_of(k * 8 * TB + n * 4 * TB, 4 * TB)
            rows = nt_dot(pick, filter_ref[pl.ds(at, 4 * TB), :].astype(BF16))
            for m in range(4):
                time_filter[8 * k + 4 * n + m] = rows[:, m * TB : (m + 1) * TB]

    vocab = iota((TB, VOCAB), 1).astype(F32)
    hot_tok = (vocab == tok_col).astype(F32).astype(BF16)
    hot_base = (vocab == as_column(base)).astype(F32).astype(BF16)

    @pl.loop(0, width // 256)
    def _(s):
        columns = pl.ds(pl.multiple_of(s * 256, 256), 256)
        part = embed_ref[:, pl.ds(pl.multiple_of(path * width + s * 256, 256), 256)]
        e_tok = jnp.dot(hot_tok, part, preferred_element_type=F32)
        e_base = jnp.dot(hot_base, part, preferred_element_type=F32)
        tok_out[:, columns] = e_tok.astype(BF16)
        base_out[:, columns] = e_base.astype(BF16)

    lane16 = iota((16, TB), 1)
    sub16 = iota((16, TB), 0)

    def shear_channel(c, _):
        before = jnp.zeros((16, TB), F32)
        for k in range(NB):
            row = jnp.broadcast_to(time_filter[k, pl.ds(c, 1), :], (16, TB))
            turned = pltpu.roll(row, 0, 1, stride=1, stride_axis=0)
            shears[c, 16 * k : 16 * k + 16, :] = jnp.where(
                lane16 >= sub16, turned, before
            ).astype(BF16)
            before = turned
        return 0

    lax.fori_loop(0, CH, shear_channel, 0)

    @pl.loop(1, NC)
    def _(d):
        dst = lax.rem(me + d, NC)
        src = lax.rem(me - d + NC, NC)
        info_copy(d, dst, src).wait_recv()
        cols_copy(d, dst, src).wait_recv()

    flip = (iota((TB, TB), 0) + iota((TB, TB), 1) == TB - 1).astype(F32).astype(BF16)
    past[...] = jnp.zeros_like(past)

    def forward(a, _):
        info = info_ref[a]
        e_tok = take_lanes(table[...], info[4:5].astype(jnp.int32))
        e_base = take_lanes(table[...], info[5:6].astype(jnp.int32))
        diff = e_tok - e_base
        e_base_s[a] = e_base
        diff_s[a] = diff
        cot = cols_ref[a].astype(F32)
        gain = coef[0]
        for p in range(NP):
            now = rounded((e_base + ALPHAS[p] * diff) * info[p : p + 1] * gain)
            one = pltpu.roll(now, 1, 1)
            two = pltpu.roll(now, 2, 1)
            now1 = jnp.where(lane < 1, past[p, 0], one)
            now2 = jnp.where(lane < 2, past[p, 1], two)
            past[p, 0] = one
            past[p, 1] = two
            q, k, v = (
                taps[f * 3] * now + taps[f * 3 + 1] * now1 + taps[f * 3 + 2] * now2
                for f in range(3)
            )
            key_s[a, p] = k
            val_s[a, p] = v
            stage[a, p * STRIDE : p * STRIDE + CH, :] = rounded(k * v)
            turn[a, p * CH : (p + 1) * CH, :] = (cot * q).astype(BF16)
        return 0

    def forward_pair(step, _):
        forward(2 * step, 0)
        forward(2 * step + 1, 0)
        return 0

    lax.fori_loop(0, NB // 2, forward_pair, 0)

    def flip_in(step, _):
        for n in range(FLIPS):
            a = step * FLIPS + n
            turned = jnp.dot(turn[a], flip, preferred_element_type=F32)
            for p in range(NP):
                at = (NP + p) * STRIDE
                stage[NB - 1 - a, at : at + CH, :] = turned[p * CH : (p + 1) * CH]
        return 0

    lax.fori_loop(0, NB // FLIPS, flip_in, 0)

    low16 = lane16 < TB // 2
    low8 = iota((8, TB), 1) < TB // 2
    zero_tile = jnp.zeros((16, TB), BF16)

    def channel(c):
        rows = pl.ds(c, 8, stride=STRIDE)
        even, odd = [], []
        data = turned_data = zero_tile
        for t in range(NB // 2):
            tile = jnp.concatenate(
                [stage[2 * t, rows, :], stage[2 * t + 1, rows, :]], 0
            ).astype(BF16)
            swapped = pltpu.roll(tile, TB // 2, 1)
            even.append(jnp.where(low16, tile, turned_data))
            odd.append(jnp.where(low16, swapped, data))
            data, turned_data = tile, swapped
        rolled = [zero_tile] * 4
        blocks = []
        acc = None
        for k in range(NB):
            shear = shears[c, 16 * k : 16 * k + 16, :]
            tiles = [shear]
            now = [shear]
            for g in range(1, 4):
                moved = pltpu.roll(shear, 16 * g, 1)
                tiles.append(jnp.where(lane16 >= 16 * g, moved, rolled[g]))
                now.append(moved)
            rolled = now
            blocks.append(jnp.concatenate(tiles, 0))
            if k % (4 * CHUNK) == 4 * CHUNK - 1:
                first = k // 4 - CHUNK + 1
                rhs = jnp.concatenate(
                    [
                        jnp.concatenate([blocks[2 * n], blocks[2 * n + 1]], 1)
                        for n in range(2 * CHUNK)
                    ],
                    0,
                )
                blocks = []
                count = NB // 2 - 2 * first
                lhs = jnp.concatenate(
                    [
                        jnp.concatenate(
                            ([zero_tile] * (2 * n) + even)[:count]
                            + ([zero_tile] * (2 * n) + odd)[:count],
                            0,
                        )
                        for n in range(CHUNK)
                    ],
                    1,
                )
                part = jnp.dot(lhs, rhs, preferred_element_type=F32)
                if acc is None:
                    acc = part
                else:
                    skip_rows = 32 * first
                    acc = jnp.concatenate(
                        [
                            acc[:skip_rows],
                            acc[skip_rows:256] + part[: 16 * count],
                            acc[256 : 256 + skip_rows],
                            acc[256 + skip_rows :] + part[16 * count :],
                        ],
                        0,
                    )
        last = jnp.zeros((8, TB), F32)
        for a in range(NB):
            out = acc[8 * a : 8 * a + 8, :TB]
            side = acc[256 + 8 * a : 264 + 8 * a, :TB]
            if a > 0:
                out = out + acc[8 * a - 8 : 8 * a, TB:]
                side = side + acc[248 + 8 * a : 256 + 8 * a, TB:]
            swapped = pltpu.roll(side, TB // 2, 1)
            conv[a, rows, :] = out + jnp.where(low8, last, swapped)
            last = swapped

    def channels(step, _):
        for n in range(UNROLL):
            channel(step * UNROLL + n)
        return 0

    lax.fori_loop(0, CH // UNROLL, channels, 0)

    ahead[...] = jnp.zeros_like(ahead)

    def flip_out(step, _):
        for n in range(FLIPS):
            a = step * FLIPS + n
            got_rows = []
            for p in range(NP):
                rows = slice((NP + p) * STRIDE, (NP + p) * STRIDE + CH)
                got_rows.append((conv[a, rows, :] + coef[1] * stage[a, rows, :]).astype(BF16))
            grad_z[NB - 1 - a] = jnp.dot(
                jnp.concatenate(got_rows, 0), flip, preferred_element_type=F32
            )
        return 0

    lax.fori_loop(0, NB // FLIPS, flip_out, 0)

    def is_self(dst):
        return (to_path == path) & (dst == me)

    def backward(step, _):
        a = lax.rem(me + 1 - step + 2 * NB, NB)
        info = info_ref[a]
        cot = cols_ref[a].astype(F32)
        e_base = e_base_s[a]
        diff = diff_s[a]
        gain = coef[0]
        skip = coef[1]
        total = jnp.zeros((CH, TB), F32)
        sum_a = jnp.zeros((CH, TB), F32)
        sum_b = jnp.zeros((CH, TB), F32)
        for p in range(NP):
            rows = slice(p * STRIDE, p * STRIDE + CH)
            out = rounded(conv[a, rows, :] + skip * stage[a, rows, :])
            gz = grad_z[a, p * CH : (p + 1) * CH, :]
            gq = rounded(cot * out)
            gk = rounded(gz * val_s[a, p])
            gv = rounded(gz * key_s[a, p])
            u0, u1, u2 = (taps[j] * gq + taps[3 + j] * gk + taps[6 + j] * gv for j in range(3))
            one = pltpu.roll(u1, TB - 1, 1)
            two = pltpu.roll(u2, TB - 2, 1)
            gn = (
                u0
                + jnp.where(lane < TB - 1, one, ahead[p, 0])
                + jnp.where(lane < TB - 2, two, ahead[p, 1])
            )
            ahead[p, 0] = one
            ahead[p, 1] = two
            inv = info[p : p + 1]
            scaled = gain * gn
            total = total + inv * scaled
            w = (e_base + ALPHAS[p] * diff) * scaled * (inv * inv * inv)
            sum_a = sum_a + w
            sum_b = sum_b + ALPHAS[p] * w

        @pl.when(step > 0)
        def _():
            sums[a] = total.astype(BF16)
            ab[a, 0:1, :] = jnp.sum(sum_a, 0, keepdims=True)
            ab[a, 1:2, :] = jnp.sum(sum_b, 0, keepdims=True)

            @pl.when(jnp.logical_not(is_self(a)))
            def _():
                ab_copy(a, slot, slot).start()
                sums_copy(a, slot, slot).start()

            @pl.when(is_self(a))
            def _():
                got[pl.ds(slot, 1)] = sums[pl.ds(a, 1)]
                got_ab[pl.ds(slot, 1)] = ab[pl.ds(a, 1)]

        @pl.when(a == 0)
        def _():
            ahead[...] = jnp.zeros_like(ahead)

        return 0

    lax.fori_loop(0, NB + 1, backward, 0)

    def others(s):
        return jnp.logical_not((to_path == path) & (s == slot))

    @pl.loop(0, NC)
    def _(s):
        @pl.when(others(s))
        def _():
            ab_copy(me, s, s).wait_recv()

    own_ab[...] = jnp.sum(got_ab[...], 0)

    @pl.loop(1, NP)
    def _(d):
        group_copy(d, path).start()

    @pl.loop(0, NC)
    def _(s):
        @pl.when(others(s))
        def _():
            sums_copy(me, s, s).wait_recv()

    both = own_ab[...]
    for d in range(1, NP):
        src = lax.rem(path - d + NP, NP)
        group_copy(d, src).wait_recv()
        both = both + group_ab[pl.ds(src, 1)][0]
    both_out[...] = both
    sums_out[...] = got[...]

    @pl.loop(1, NC)
    def _(d):
        dst = lax.rem(me + d, NC)
        info_copy(d, dst, me).wait_send()
        cols_copy(d, dst, me).wait_send()

    @pl.loop(0, NC)
    def _(d):
        @pl.when(jnp.logical_not(is_self(d)))
        def _():
            ab_copy(d, slot, slot).wait_send()
            sums_copy(d, slot, slot).wait_send()

    @pl.loop(1, NP)
    def _(d):
        group_copy(d, path).wait_send()


def output_kernel(sums_ref, both_ref, tok_ref, base_ref, grad_ref, attr_ref):
    eye = iota((TB, TB), 0) == iota((TB, TB), 1)
    unit = eye.astype(F32).astype(BF16)
    scale = 1.0 / (NP * D)

    def as_column(row):
        return jnp.sum(jnp.where(eye, row, 0.0), 1, keepdims=True) * scale

    a_col = as_column(both_ref[0:1])
    b_col = as_column(both_ref[1:2])
    for n in range(OUT // TB):
        columns = slice(n * TB, (n + 1) * TB)
        summed = nt_dot(unit, sums_ref[4 * n : 4 * n + 4].reshape(TB, TB))
        e_base = base_ref[:, columns].astype(F32)
        diff = tok_ref[:, columns].astype(F32) - e_base
        grad = summed * (1.0 / NP) - (e_base * a_col + diff * b_col)
        grad_ref[:, columns] = grad
        attr_ref[:, columns] = diff * grad


def body(tokens, sub_pos, sub_base, embed, norm_gain, fir_taps, long_filter, skip_gain, cotangent):
    vmem = pl.BlockSpec(memory_space=pltpu.VMEM)
    here = pl.BlockSpec(memory_space=pl.ANY)
    width = D // NP
    rows = jax.ShapeDtypeStruct((TB, width), BF16)
    dma = pltpu.SemaphoreType.DMA
    sums, both, e_tok, e_base = pl.pallas_call(
        fused_kernel,
        name="fused_stage",
        out_shape=(
            jax.ShapeDtypeStruct((NC, CH, TB), BF16),
            jax.ShapeDtypeStruct((2, TB), F32),
            rows,
            rows,
        ),
        in_specs=[vmem, vmem, vmem, here, vmem, vmem, here, vmem, here],
        out_specs=(vmem, vmem, vmem, vmem),
        scratch_shapes=[
            pltpu.VMEM((VOCAB, D), BF16),
            pltpu.VMEM((NB * TB, TB), F32),
            pltpu.VMEM((TB, D), BF16),
            pltpu.VMEM((8, TB), F32),
            pltpu.VMEM((NC, CH, TB), BF16),
            pltpu.VMEM((NC, 8, TB), F32),
            pltpu.VMEM((NC, CH, TB), BF16),
            pltpu.VMEM((CH, VOCAB), F32),
            pltpu.VMEM((9, CH, TB), F32),
            pltpu.VMEM((2, CH, TB), F32),
            pltpu.VMEM((NB, CH, TB), F32),
            pltpu.VMEM((NB, CH, TB), F32),
            pltpu.VMEM((NB, CH, TB), F32),
            pltpu.VMEM((NB, NP, CH, TB), F32),
            pltpu.VMEM((NB, NP, CH, TB), F32),
            pltpu.VMEM((NB, 2 * NP * STRIDE, TB), F32),
            pltpu.VMEM((NB, 2 * NP * STRIDE, TB), F32),
            pltpu.VMEM((NP, 2, CH, TB), F32),
            pltpu.VMEM((NP, 2, CH, TB), F32),
            pltpu.VMEM((NC, CH, TB), BF16),
            pltpu.VMEM((NC, 2, TB), F32),
            pltpu.VMEM((NC, CH, TB), BF16),
            pltpu.VMEM((NC, 2, TB), F32),
            pltpu.VMEM((2, TB), F32),
            pltpu.VMEM((NP, 2, TB), F32),
            pltpu.VMEM((NB, NP * CH, TB), BF16),
            pltpu.VMEM((NB, NP * CH, TB), F32),
            pltpu.VMEM((CH, NB * 16, TB), BF16),
            dma((3,)),
            dma((NC,)),
            dma((NC,)),
            dma((NC,)),
            dma((NC,)),
            dma((NC,)),
            dma((NC,)),
            dma((NC,)),
            dma((NC,)),
            dma((NP,)),
            dma((NP,)),
        ],
        compiler_params=pltpu.CompilerParams(
            collective_id=0, has_side_effects=True, vmem_limit_bytes=VMEM_LIMIT
        ),
    )(
        tokens.reshape(1, -1),
        sub_pos.reshape(1, -1),
        sub_base.reshape(1, -1),
        embed,
        norm_gain.reshape(-1, TB),
        fir_taps,
        long_filter,
        skip_gain.reshape(1, -1),
        cotangent,
    )
    block = pl.BlockSpec((TB, OUT), lambda i: (0, i))
    shape = jax.ShapeDtypeStruct((TB, width), F32)
    return pl.pallas_call(
        output_kernel,
        name="output_stage",
        grid=(width // OUT,),
        out_shape=(shape, shape),
        in_specs=[
            pl.BlockSpec((OUT // CH, CH, TB), lambda i: (i, 0, 0)),
            pl.BlockSpec((2, TB), lambda i: (0, 0)),
            block,
            block,
        ],
        out_specs=(block, block),
    )(sums, both, e_tok, e_base)


def solution(mesh):
    return jax.shard_map(
        body,
        mesh=mesh,
        in_specs=(
            P("ctx"),
            P("ctx"),
            P("ctx"),
            P(),
            P(),
            P(),
            P(None, "ctx"),
            P("ctx"),
            P("ctx", None),
        ),
        out_specs=(P("ctx", "path"), P("ctx", "path")),
        check_vma=False,
    )
```

```python
import jax
import jax.numpy as jnp
from jax import lax
from jax.experimental import pallas as pl
from jax.experimental.pallas import tpu as pltpu
from jax.sharding import PartitionSpec as P

MESH = pl.DeviceIdType.MESH
F32 = jnp.float32
BF16 = jnp.bfloat16

NP = 4
NC = 32
TB = 128
CH = 32
NB = 32
SUB = 16
VOCAB = 512
D = 4096
REACH = 2
STRIDE = CH + 1
UNROLL = 8
CHUNK = 2
FLIPS = 8
OUT = 512
ALPHAS = tuple((a + 0.5) / NP for a in range(NP))
VMEM_LIMIT = 60 * 1024 * 1024


def iota(shape, dim):
    return lax.broadcasted_iota(jnp.int32, shape, dim)


def rounded(x):
    return x.astype(BF16).astype(F32)


def nt_dot(a, b):
    return lax.dot_general(a, b, (((1,), (1,)), ((), ())), preferred_element_type=F32)


def take_lanes(table, index):
    rows = table.shape[0]
    low = jnp.broadcast_to(index & (TB - 1), (8, TB))
    high = jnp.broadcast_to(index >> 7, (8, TB))
    out = []
    for r in range(0, rows, 8):
        got = jnp.take_along_axis(table[r : r + 8, :TB], low, axis=1)
        for v in range(1, VOCAB // TB):
            more = jnp.take_along_axis(table[r : r + 8, v * TB : (v + 1) * TB], low, axis=1)
            got = jnp.where(high == v, more, got)
        out.append(got)
    return jnp.concatenate(out, 0)


def fused_kernel(
    tok_ref,
    sub_pos_ref,
    sub_base_ref,
    embed_hbm,
    gain_ref,
    taps_ref,
    filter_hbm,
    skip_ref,
    cot_hbm,
    sums_out,
    both_out,
    tok_out,
    base_out,
    embed_ref,
    filter_ref,
    cot_ref,
    mine,
    parts,
    info_ref,
    cols_ref,
    table,
    taps,
    coef,
    time_filter,
    e_base_s,
    diff_s,
    key_s,
    val_s,
    stage,
    conv,
    past,
    ahead,
    sums,
    ab,
    got,
    got_ab,
    own_ab,
    group_ab,
    turn,
    grad_z,
    shears,
    load_sem,
    info_send,
    info_recv,
    cols_send,
    cols_recv,
    sums_send,
    sums_recv,
    ab_send,
    ab_recv,
    group_send,
    group_recv,
):
    path = lax.axis_index("path")
    me = lax.axis_index("ctx")
    width = D // NP
    to_path = me // 8
    slot = (me % 8) * NP + path
    own = jnp.where(to_path == path, 1, 0)

    def partner(ctx):
        return jnp.where(ctx // 4 % 2 == me // 4 % 2, path, lax.rem(path + 2, NP))

    load_cot = pltpu.make_async_copy(cot_hbm, cot_ref, load_sem.at[0])
    load_embed = pltpu.make_async_copy(embed_hbm, embed_ref, load_sem.at[1])
    load_filter = pltpu.make_async_copy(filter_hbm, filter_ref, load_sem.at[2])
    load_cot.start()
    load_embed.start()
    load_filter.start()

    barrier = pltpu.get_barrier_semaphore()

    @pl.loop(1, NC)
    def _(d):
        other = lax.rem(me + d, NC)
        pl.semaphore_signal(
            barrier,
            inc=1,
            device_id={"path": partner(other), "ctx": other},
            device_id_type=MESH,
        )

    @pl.loop(0, NC)
    def _(s):
        src_path = lax.rem(s, NP)
        src_ctx = path * 8 + s // NP

        @pl.when((src_path != path) | (src_ctx != me))
        def _():
            pl.semaphore_signal(
                barrier,
                inc=1,
                device_id={"path": src_path, "ctx": src_ctx},
                device_id_type=MESH,
            )

    @pl.loop(1, NP)
    def _(d):
        pl.semaphore_signal(
            barrier, inc=1, device_id={"path": lax.rem(path + d, NP)}, device_id_type=MESH
        )

    def cols_copy(d, dst, at):
        return pltpu.make_async_remote_copy(
            src_ref=parts.at[dst],
            dst_ref=cols_ref.at[at],
            send_sem=cols_send.at[d],
            recv_sem=cols_recv.at[d],
            device_id={"path": partner(dst), "ctx": dst},
            device_id_type=MESH,
        )

    def info_copy(d, dst, at):
        return pltpu.make_async_remote_copy(
            src_ref=mine,
            dst_ref=info_ref.at[at],
            send_sem=info_send.at[d],
            recv_sem=info_recv.at[d],
            device_id={"path": partner(dst), "ctx": dst},
            device_id_type=MESH,
        )

    def sums_copy(dst, at, number):
        return pltpu.make_async_remote_copy(
            src_ref=sums.at[dst],
            dst_ref=got.at[at],
            send_sem=sums_send.at[dst],
            recv_sem=sums_recv.at[number],
            device_id={"path": to_path, "ctx": dst},
            device_id_type=MESH,
        )

    def ab_copy(dst, at, number):
        return pltpu.make_async_remote_copy(
            src_ref=ab.at[dst],
            dst_ref=got_ab.at[at],
            send_sem=ab_send.at[dst],
            recv_sem=ab_recv.at[number],
            device_id={"path": to_path, "ctx": dst},
            device_id_type=MESH,
        )

    def group_copy(d, at):
        return pltpu.make_async_remote_copy(
            src_ref=own_ab,
            dst_ref=group_ab.at[at],
            send_sem=group_send.at[d],
            recv_sem=group_recv.at[d],
            device_id={"path": lax.rem(path + d, NP)},
            device_id_type=MESH,
        )

    lane = iota((CH, TB), 1)
    chosen = lane == iota((CH, TB), 0) + path * CH
    pick = chosen.astype(F32).astype(BF16)
    load_cot.wait()

    @pl.loop(0, NC // 4)
    def _(step):
        to = partner(4 * step)
        want = (lane == iota((CH, TB), 0) + to * CH).astype(F32).astype(BF16)
        for n in range(4):
            block = cot_ref[:, pl.ds(pl.multiple_of((4 * step + n) * TB, TB), TB)]
            parts[4 * step + n] = nt_dot(want, block).astype(BF16)

    cols_ref[pl.ds(me, 1)] = parts[pl.ds(me, 1)]

    tok = tok_ref[...].astype(F32)
    diag = iota((SUB, SUB), 0) == iota((SUB, SUB), 1)
    pos_row = (sub_pos_ref[...] & 7).astype(F32)
    pos_col = jnp.sum(jnp.where(diag, pos_row, 0.0), 1, keepdims=True) + 8.0 * iota(
        (SUB, 1), 0
    ).astype(F32)
    base_col = jnp.sum(jnp.where(diag, sub_base_ref[...].astype(F32), 0.0), 1, keepdims=True)
    at_sub = iota((SUB, TB), 1).astype(F32) == pos_col
    covered = jnp.sum(jnp.where(at_sub, 1.0, 0.0), 0, keepdims=True) > 0.5
    base = jnp.where(covered, jnp.sum(jnp.where(at_sub, base_col, 0.0), 0, keepdims=True), tok)
    sub_tok_col = jnp.sum(jnp.where(at_sub, tok, 0.0), 1, keepdims=True)
    eye = iota((TB, TB), 0) == iota((TB, TB), 1)

    def as_column(row):
        return jnp.sum(jnp.where(eye, row, 0.0), 1, keepdims=True)

    tok_col = as_column(tok)
    ids = jnp.concatenate([tok_col, sub_tok_col, base_col], 0)
    hot = (iota((TB + 2 * SUB, VOCAB), 1).astype(F32) == ids).astype(F32).astype(BF16)
    load_embed.wait()

    def squares(step, carry):
        plain, subs = carry
        for n in range(2):
            part = embed_ref[:, pl.ds(pl.multiple_of(step * 512 + n * 256, 256), 256)]
            found = jnp.dot(hot, part, preferred_element_type=F32)
            plain_rows = found[:TB]
            plain_rows = plain_rows * plain_rows
            plain = plain + (plain_rows[:, :TB] + plain_rows[:, TB:])
            e_tok = found[TB : TB + SUB]
            e_base = found[TB + SUB :]
            diff = e_tok - e_base
            new = []
            for a in range(NP):
                x = e_base + ALPHAS[a] * diff
                x = x * x
                new.append(subs[a] + (x[:, :TB] + x[:, TB:]))
            subs = tuple(new)
        return plain, subs

    plain, subs = lax.fori_loop(
        0,
        D // 512,
        squares,
        (jnp.zeros((TB, TB), F32), tuple(jnp.zeros((SUB, TB), F32) for _ in range(NP))),
    )

    def inverse(total):
        return lax.rsqrt(jnp.sum(total, 1, keepdims=True) / D + 1e-06)

    plain_row = jnp.sum(jnp.where(eye, inverse(plain), 0.0), 0, keepdims=True)
    for a in range(NP):
        sub_row = jnp.sum(jnp.where(at_sub, inverse(subs[a]), 0.0), 0, keepdims=True)
        mine[a : a + 1, :] = jnp.where(covered, sub_row, plain_row)
    mine[4:5, :] = tok
    mine[5:6, :] = base
    mine[6:8, :] = jnp.zeros((2, TB), F32)
    info_ref[pl.ds(me, 1)] = mine[...].reshape(1, 8, TB)

    pl.semaphore_wait(barrier, 2 * NC + NP - 2 - own)

    @pl.loop(1, NC)
    def _(d):
        info_copy(d, lax.rem(me + d, NC), me).start()
        cols_copy(d, lax.rem(me + d, NC), me).start()

    lanes = pl.ds(pl.multiple_of(me * TB, TB), TB)

    def column(row):
        return jnp.broadcast_to(
            jnp.sum(jnp.where(chosen, row, 0.0), 1, keepdims=True), (CH, TB)
        )

    coef[0] = column(gain_ref[pl.ds(me, 1), :])
    coef[1] = column(skip_ref[...])
    for f in range(3):
        for j in range(3):
            taps[f * 3 + j] = column(taps_ref[f, j : j + 1, lanes].astype(F32))
    table[...] = nt_dot(pick, embed_ref[:, lanes])
    load_filter.wait()

    @pl.loop(0, NB // 8)
    def _(k):
        for n in range(2):
            at = pl.multiple_of(k * 8 * TB + n * 4 * TB, 4 * TB)
            rows = nt_dot(pick, filter_ref[pl.ds(at, 4 * TB), :].astype(BF16))
            for m in range(4):
                time_filter[8 * k + 4 * n + m] = rows[:, m * TB : (m + 1) * TB]

    vocab = iota((TB, VOCAB), 1).astype(F32)
    hot_tok = (vocab == tok_col).astype(F32).astype(BF16)
    hot_base = (vocab == as_column(base)).astype(F32).astype(BF16)

    @pl.loop(0, width // 256)
    def _(s):
        columns = pl.ds(pl.multiple_of(s * 256, 256), 256)
        part = embed_ref[:, pl.ds(pl.multiple_of(path * width + s * 256, 256), 256)]
        e_tok = jnp.dot(hot_tok, part, preferred_element_type=F32)
        e_base = jnp.dot(hot_base, part, preferred_element_type=F32)
        tok_out[:, columns] = e_tok.astype(BF16)
        base_out[:, columns] = e_base.astype(BF16)

    lane16 = iota((16, TB), 1)
    sub16 = iota((16, TB), 0)

    def shear_channel(c, _):
        before = jnp.zeros((16, TB), F32)
        for k in range(NB):
            row = jnp.broadcast_to(time_filter[k, pl.ds(c, 1), :], (16, TB))
            turned = pltpu.roll(row, 0, 1, stride=1, stride_axis=0)
            shears[c, 16 * k : 16 * k + 16, :] = jnp.where(
                lane16 >= sub16, turned, before
            ).astype(BF16)
            before = turned
        return 0

    lax.fori_loop(0, CH, shear_channel, 0)

    @pl.loop(1, NC)
    def _(d):
        dst = lax.rem(me + d, NC)
        src = lax.rem(me - d + NC, NC)
        info_copy(d, dst, src).wait_recv()
        cols_copy(d, dst, src).wait_recv()

    flip = (iota((TB, TB), 0) + iota((TB, TB), 1) == TB - 1).astype(F32).astype(BF16)
    past[...] = jnp.zeros_like(past)

    def forward(a, _):
        info = info_ref[a]
        e_tok = take_lanes(table[...], info[4:5].astype(jnp.int32))
        e_base = take_lanes(table[...], info[5:6].astype(jnp.int32))
        diff = e_tok - e_base
        e_base_s[a] = e_base
        diff_s[a] = diff
        cot = cols_ref[a].astype(F32)
        gain = coef[0]
        for p in range(NP):
            now = rounded((e_base + ALPHAS[p] * diff) * info[p : p + 1] * gain)
            one = pltpu.roll(now, 1, 1)
            two = pltpu.roll(now, 2, 1)
            now1 = jnp.where(lane < 1, past[p, 0], one)
            now2 = jnp.where(lane < 2, past[p, 1], two)
            past[p, 0] = one
            past[p, 1] = two
            q, k, v = (
                taps[f * 3] * now + taps[f * 3 + 1] * now1 + taps[f * 3 + 2] * now2
                for f in range(3)
            )
            key_s[a, p] = k
            val_s[a, p] = v
            stage[a, p * STRIDE : p * STRIDE + CH, :] = rounded(k * v)
            turn[a, p * CH : (p + 1) * CH, :] = (cot * q).astype(BF16)
        return 0

    def forward_blocks(step, _):
        for n in range(4):
            forward(4 * step + n, 0)
        return 0

    lax.fori_loop(0, NB // 4, forward_blocks, 0)

    def flip_in(step, _):
        for n in range(FLIPS):
            a = step * FLIPS + n
            turned = jnp.dot(turn[a], flip, preferred_element_type=F32)
            for p in range(NP):
                at = (NP + p) * STRIDE
                stage[NB - 1 - a, at : at + CH, :] = turned[p * CH : (p + 1) * CH]
        return 0

    lax.fori_loop(0, NB // FLIPS, flip_in, 0)

    low16 = lane16 < TB // 2
    low8 = iota((8, TB), 1) < TB // 2
    zero_tile = jnp.zeros((16, TB), BF16)

    def channel(c):
        rows = pl.ds(c, 8, stride=STRIDE)
        even, odd = [], []
        data = turned_data = zero_tile
        for t in range(NB // 2):
            tile = jnp.concatenate(
                [stage[2 * t, rows, :], stage[2 * t + 1, rows, :]], 0
            ).astype(BF16)
            swapped = pltpu.roll(tile, TB // 2, 1)
            even.append(jnp.where(low16, tile, turned_data))
            odd.append(jnp.where(low16, swapped, data))
            data, turned_data = tile, swapped
        rolled = [zero_tile] * 4
        blocks = []
        acc = None
        for k in range(NB):
            shear = shears[c, 16 * k : 16 * k + 16, :]
            tiles = [shear]
            now = [shear]
            for g in range(1, 4):
                moved = pltpu.roll(shear, 16 * g, 1)
                tiles.append(jnp.where(lane16 >= 16 * g, moved, rolled[g]))
                now.append(moved)
            rolled = now
            blocks.append(jnp.concatenate(tiles, 0))
            if k % (4 * CHUNK) == 4 * CHUNK - 1:
                first = k // 4 - CHUNK + 1
                rhs = jnp.concatenate(
                    [
                        jnp.concatenate([blocks[2 * n], blocks[2 * n + 1]], 1)
                        for n in range(2 * CHUNK)
                    ],
                    0,
                )
                blocks = []
                count = NB // 2 - 2 * first
                lhs = jnp.concatenate(
                    [
                        jnp.concatenate(
                            ([zero_tile] * (2 * n) + even)[:count]
                            + ([zero_tile] * (2 * n) + odd)[:count],
                            0,
                        )
                        for n in range(CHUNK)
                    ],
                    1,
                )
                part = jnp.dot(lhs, rhs, preferred_element_type=F32)
                if acc is None:
                    acc = part
                else:
                    skip_rows = 32 * first
                    acc = jnp.concatenate(
                        [
                            acc[:skip_rows],
                            acc[skip_rows:256] + part[: 16 * count],
                            acc[256 : 256 + skip_rows],
                            acc[256 + skip_rows :] + part[16 * count :],
                        ],
                        0,
                    )
        last = jnp.zeros((8, TB), F32)
        for a in range(NB):
            out = acc[8 * a : 8 * a + 8, :TB]
            side = acc[256 + 8 * a : 264 + 8 * a, :TB]
            if a > 0:
                out = out + acc[8 * a - 8 : 8 * a, TB:]
                side = side + acc[248 + 8 * a : 256 + 8 * a, TB:]
            swapped = pltpu.roll(side, TB // 2, 1)
            conv[a, rows, :] = out + jnp.where(low8, last, swapped)
            last = swapped

    def channels(step, _):
        for n in range(UNROLL):
            channel(step * UNROLL + n)
        return 0

    lax.fori_loop(0, CH // UNROLL, channels, 0)

    ahead[...] = jnp.zeros_like(ahead)

    def flip_out(step, _):
        for n in range(FLIPS):
            a = step * FLIPS + n
            got_rows = []
            for p in range(NP):
                rows = slice((NP + p) * STRIDE, (NP + p) * STRIDE + CH)
                got_rows.append((conv[a, rows, :] + coef[1] * stage[a, rows, :]).astype(BF16))
            grad_z[NB - 1 - a] = jnp.dot(
                jnp.concatenate(got_rows, 0), flip, preferred_element_type=F32
            )
        return 0

    lax.fori_loop(0, NB // FLIPS, flip_out, 0)

    def is_self(dst):
        return (to_path == path) & (dst == me)

    def backward(step, _):
        a = lax.rem(me + 1 - step + 2 * NB, NB)
        info = info_ref[a]
        cot = cols_ref[a].astype(F32)
        e_base = e_base_s[a]
        diff = diff_s[a]
        gain = coef[0]
        skip = coef[1]
        total = jnp.zeros((CH, TB), F32)
        sum_a = jnp.zeros((CH, TB), F32)
        sum_b = jnp.zeros((CH, TB), F32)
        for p in range(NP):
            rows = slice(p * STRIDE, p * STRIDE + CH)
            out = rounded(conv[a, rows, :] + skip * stage[a, rows, :])
            gz = grad_z[a, p * CH : (p + 1) * CH, :]
            gq = rounded(cot * out)
            gk = rounded(gz * val_s[a, p])
            gv = rounded(gz * key_s[a, p])
            u0, u1, u2 = (taps[j] * gq + taps[3 + j] * gk + taps[6 + j] * gv for j in range(3))
            one = pltpu.roll(u1, TB - 1, 1)
            two = pltpu.roll(u2, TB - 2, 1)
            gn = (
                u0
                + jnp.where(lane < TB - 1, one, ahead[p, 0])
                + jnp.where(lane < TB - 2, two, ahead[p, 1])
            )
            ahead[p, 0] = one
            ahead[p, 1] = two
            inv = info[p : p + 1]
            scaled = gain * gn
            total = total + inv * scaled
            w = (e_base + ALPHAS[p] * diff) * scaled * (inv * inv * inv)
            sum_a = sum_a + w
            sum_b = sum_b + ALPHAS[p] * w

        @pl.when(step > 0)
        def _():
            sums[a] = total.astype(BF16)
            ab[a, 0:1, :] = jnp.sum(sum_a, 0, keepdims=True)
            ab[a, 1:2, :] = jnp.sum(sum_b, 0, keepdims=True)

            @pl.when(jnp.logical_not(is_self(a)))
            def _():
                ab_copy(a, slot, slot).start()
                sums_copy(a, slot, slot).start()

            @pl.when(is_self(a))
            def _():
                got[pl.ds(slot, 1)] = sums[pl.ds(a, 1)]
                got_ab[pl.ds(slot, 1)] = ab[pl.ds(a, 1)]

        @pl.when(a == 0)
        def _():
            ahead[...] = jnp.zeros_like(ahead)

        return 0

    lax.fori_loop(0, NB + 1, backward, 0)

    def others(s):
        return jnp.logical_not((to_path == path) & (s == slot))

    @pl.loop(0, NC)
    def _(s):
        @pl.when(others(s))
        def _():
            ab_copy(me, s, s).wait_recv()

    own_ab[...] = jnp.sum(got_ab[...], 0)

    @pl.loop(1, NP)
    def _(d):
        group_copy(d, path).start()

    @pl.loop(0, NC)
    def _(s):
        @pl.when(others(s))
        def _():
            sums_copy(me, s, s).wait_recv()

    both = own_ab[...]
    for d in range(1, NP):
        src = lax.rem(path - d + NP, NP)
        group_copy(d, src).wait_recv()
        both = both + group_ab[pl.ds(src, 1)][0]
    both_out[...] = both
    sums_out[...] = got[...]

    @pl.loop(1, NC)
    def _(d):
        dst = lax.rem(me + d, NC)
        info_copy(d, dst, me).wait_send()
        cols_copy(d, dst, me).wait_send()

    @pl.loop(0, NC)
    def _(d):
        @pl.when(jnp.logical_not(is_self(d)))
        def _():
            ab_copy(d, slot, slot).wait_send()
            sums_copy(d, slot, slot).wait_send()

    @pl.loop(1, NP)
    def _(d):
        group_copy(d, path).wait_send()


def output_kernel(sums_ref, both_ref, tok_ref, base_ref, grad_ref, attr_ref):
    eye = iota((TB, TB), 0) == iota((TB, TB), 1)
    unit = eye.astype(F32).astype(BF16)
    scale = 1.0 / (NP * D)

    def as_column(row):
        return jnp.sum(jnp.where(eye, row, 0.0), 1, keepdims=True) * scale

    a_col = as_column(both_ref[0:1])
    b_col = as_column(both_ref[1:2])
    for n in range(OUT // TB):
        columns = slice(n * TB, (n + 1) * TB)
        summed = nt_dot(unit, sums_ref[4 * n : 4 * n + 4].reshape(TB, TB))
        e_base = base_ref[:, columns].astype(F32)
        diff = tok_ref[:, columns].astype(F32) - e_base
        grad = summed * (1.0 / NP) - (e_base * a_col + diff * b_col)
        grad_ref[:, columns] = grad
        attr_ref[:, columns] = diff * grad


def body(tokens, sub_pos, sub_base, embed, norm_gain, fir_taps, long_filter, skip_gain, cotangent):
    vmem = pl.BlockSpec(memory_space=pltpu.VMEM)
    here = pl.BlockSpec(memory_space=pl.ANY)
    width = D // NP
    rows = jax.ShapeDtypeStruct((TB, width), BF16)
    dma = pltpu.SemaphoreType.DMA
    sums, both, e_tok, e_base = pl.pallas_call(
        fused_kernel,
        name="fused_stage",
        out_shape=(
            jax.ShapeDtypeStruct((NC, CH, TB), BF16),
            jax.ShapeDtypeStruct((2, TB), F32),
            rows,
            rows,
        ),
        in_specs=[vmem, vmem, vmem, here, vmem, vmem, here, vmem, here],
        out_specs=(vmem, vmem, vmem, vmem),
        scratch_shapes=[
            pltpu.VMEM((VOCAB, D), BF16),
            pltpu.VMEM((NB * TB, TB), F32),
            pltpu.VMEM((TB, D), BF16),
            pltpu.VMEM((8, TB), F32),
            pltpu.VMEM((NC, CH, TB), BF16),
            pltpu.VMEM((NC, 8, TB), F32),
            pltpu.VMEM((NC, CH, TB), BF16),
            pltpu.VMEM((CH, VOCAB), F32),
            pltpu.VMEM((9, CH, TB), F32),
            pltpu.VMEM((2, CH, TB), F32),
            pltpu.VMEM((NB, CH, TB), F32),
            pltpu.VMEM((NB, CH, TB), F32),
            pltpu.VMEM((NB, CH, TB), F32),
            pltpu.VMEM((NB, NP, CH, TB), F32),
            pltpu.VMEM((NB, NP, CH, TB), F32),
            pltpu.VMEM((NB, 2 * NP * STRIDE, TB), F32),
            pltpu.VMEM((NB, 2 * NP * STRIDE, TB), F32),
            pltpu.VMEM((NP, 2, CH, TB), F32),
            pltpu.VMEM((NP, 2, CH, TB), F32),
            pltpu.VMEM((NC, CH, TB), BF16),
            pltpu.VMEM((NC, 2, TB), F32),
            pltpu.VMEM((NC, CH, TB), BF16),
            pltpu.VMEM((NC, 2, TB), F32),
            pltpu.VMEM((2, TB), F32),
            pltpu.VMEM((NP, 2, TB), F32),
            pltpu.VMEM((NB, NP * CH, TB), BF16),
            pltpu.VMEM((NB, NP * CH, TB), F32),
            pltpu.VMEM((CH, NB * 16, TB), BF16),
            dma((3,)),
            dma((NC,)),
            dma((NC,)),
            dma((NC,)),
            dma((NC,)),
            dma((NC,)),
            dma((NC,)),
            dma((NC,)),
            dma((NC,)),
            dma((NP,)),
            dma((NP,)),
        ],
        compiler_params=pltpu.CompilerParams(
            collective_id=0, has_side_effects=True, vmem_limit_bytes=VMEM_LIMIT
        ),
    )(
        tokens.reshape(1, -1),
        sub_pos.reshape(1, -1),
        sub_base.reshape(1, -1),
        embed,
        norm_gain.reshape(-1, TB),
        fir_taps,
        long_filter,
        skip_gain.reshape(1, -1),
        cotangent,
    )
    block = pl.BlockSpec((TB, OUT), lambda i: (0, i))
    shape = jax.ShapeDtypeStruct((TB, width), F32)
    return pl.pallas_call(
        output_kernel,
        name="output_stage",
        grid=(width // OUT,),
        out_shape=(shape, shape),
        in_specs=[
            pl.BlockSpec((OUT // CH, CH, TB), lambda i: (i, 0, 0)),
            pl.BlockSpec((2, TB), lambda i: (0, 0)),
            block,
            block,
        ],
        out_specs=(block, block),
    )(sums, both, e_tok, e_base)


def solution(mesh):
    return jax.shard_map(
        body,
        mesh=mesh,
        in_specs=(
            P("ctx"),
            P("ctx"),
            P("ctx"),
            P(),
            P(),
            P(),
            P(None, "ctx"),
            P("ctx"),
            P("ctx", None),
        ),
        out_specs=(P("ctx", "path"), P("ctx", "path")),
        check_vma=False,
    )
```
